256 devices in a mesh: gx: 128 (over x, y, z), gy: 2 (over core).
Axes of the slice: x: 4, y: 4, z: 8, core: 2. Of those that a mesh axis runs over, the one named last changes fastest.
Arguments:
- embeddings: bfloat16 [114688, 1024], P(('gx', 'gy')), may hold values from -16 to 16
- cluster: int32 [114688, 1], P(('gx', 'gy')), may hold values from 0 to 127; in each aligned block of 448 rows (0 to 447, 448 to 895, ...) at most 7 rows name the same one
Outputs:
- density: float32 [114688], P(('gx', 'gy'))
The draws below stay inside these ranges and needn't reach their ends.
Inputs may be any that keep to these rules, and one draw needn't show every extreme that they name: Within each aligned block of 448 rows (the rows of one device) no cluster id appears more than 7 times, and some id appears exactly 7 times.
All inputs are finite; a program needn't handle non-finite values.
Results may differ from the reference program's by a relative error of at most 0.0003.
Values may be sent and summed in bfloat16 or wider, within the bound.
No kernel may reach another device: no remote copies, remote signals or barrier semaphores. Data moves between devices by JAX's collectives and lax.ppermute only.
A program may use at most 64 MiB of HBM per device.

```python
import math
import jax
import jax.numpy as jnp
import numpy as np
from jax import lax

D = 1024
ROWS_DEV = 448
CLUSTERS = 128
CAP = 7
GROUP_SLOTS = 1792
TOTAL = 114688
DEVICES = 256


topic_count = 64


def draw_embeddings(key, part):
    topic_key, centre_key, gain_key, amp_key, noise_key, spread_key = jax.random.split(key, 6)
    topics = jax.random.randint(topic_key, (TOTAL,), 0, topic_count)
    centres = jax.random.normal(centre_key, (topic_count, D), jnp.float32) * (2.0 * D ** (-0.25))
    amps = jax.random.uniform(amp_key, (TOTAL,), jnp.float32, 0.5, 1.5)
    spread = jnp.exp(jax.random.uniform(spread_key, (TOTAL,), jnp.float32, math.log(0.3), math.log(1.2)))
    gains = jnp.exp(jax.random.uniform(gain_key, (topic_count,), jnp.float32, math.log(0.7), math.log(1.4)))
    noise = jnp.clip(jax.random.normal(noise_key, (TOTAL, D), jnp.float32), -4.0, 4.0)
    row_gain = jnp.take(gains, topics, axis=0) * amps
    row_centre = jnp.take(centres, topics, axis=0)
    values = row_gain[:, None] * row_centre + spread[:, None] * noise
    return jnp.clip(values, -16.0, 16.0).astype(jnp.bfloat16)


def assign_block(own_key, own, number, rows, number_of, top, bound, skew):
    order = jax.random.permutation(own_key, number_of)
    packed, common = load_shares(number_of, rows * top, bound, skew, True), load_shares(number_of, rows * top, bound, skew, False)
    places = jnp.arange(number_of)

    def named(tallies, offset_by):
        used = int((tallies > 0).sum())
        fixed = max(1, used // 4)
        moved = fixed + (places - fixed + offset_by * (used - fixed)) % max(1, number_of - fixed)
        return jnp.zeros((number_of,), jnp.int32).at[order[jnp.where(places < fixed, places, moved)]].set(jnp.asarray(tallies, jnp.int32))

    tallies = jnp.where(number % 4 == 0, named(packed, number // 4), named(common, number - number // 4 - 1))
    mixed = jax.random.permutation(jax.random.fold_in(own, 3), number_of)
    giver, taker = mixed[0:number_of // 2 * 2:2], mixed[1:number_of // 2 * 2:2]
    margin = jnp.minimum(tallies[giver] - 1, bound - tallies[taker]) // 2
    margin = jnp.where((giver == order[0]) | (taker == order[0]) | (tallies[taker] == 0), 0, jnp.maximum(margin, 0))
    moved = jax.random.randint(jax.random.fold_in(own, 4), (number_of // 2,), 0, 1 << 20) % (margin + 1)
    tallies = tallies.at[giver].add(-moved).at[taker].add(moved)
    items = jnp.searchsorted(jnp.cumsum(tallies), jnp.arange(rows * top), side="right").astype(jnp.int32)
    grid = items.reshape(top, rows).T
    grid = grid[jax.random.permutation(jax.random.fold_in(own, 1), rows)]
    offset_by = jax.random.randint(jax.random.fold_in(own, 2), (rows, 1), 0, top)
    return jnp.take_along_axis(grid, (jnp.arange(top)[None, :] + offset_by) % top, axis=1)


def load_shares(amount, total, reach, slope, full):
    portions = [(1 << 20) // math.isqrt(grade ** slope) + 1 for grade in range(1, amount + 1)]
    largest = reach if full else min(reach, max(-(-total // amount), total * portions[0] // sum(portions)))
    least = 1 if total - largest >= amount - 1 else 0
    given, surplus = [largest] + [least] * (amount - 1), total - largest - least * (amount - 1)
    while surplus > 0:
        free = [i for i in range(1, amount) if given[i] < largest] or [i for i in range(1, amount) if given[i] < reach]
        pool, budget = sum([portions[i] for i in free]), surplus
        for i in free:
            addition = min(reach - given[i], max(1, budget * portions[i] // pool), surplus)
            given[i] = given[i] + addition
            surplus = surplus - addition
    return np.array(given)


def setup_inputs(seed: int = 0) -> dict:
    seeds = jax.random.split(jax.random.key(seed), 3)
    embeddings = draw_embeddings(jax.random.fold_in(seeds[2], 71), 0)
    cluster_keys = jax.random.split(jax.random.fold_in(seeds[1], 1), TOTAL // ROWS_DEV)
    cluster_turns = jax.random.permutation(jax.random.fold_in(seeds[1], 3), TOTAL // ROWS_DEV)
    cluster = jax.vmap(lambda own, number: assign_block(jax.random.fold_in(seeds[1], 2), own, number, ROWS_DEV, CLUSTERS, 1, CAP, 2))(cluster_keys, cluster_turns).reshape((TOTAL, 1))
    return dict(embeddings=embeddings, cluster=cluster)


prior_score = math.log(64.0)


def reference(embeddings, cluster):
    cluster_ids = cluster[:, 0]
    blocks = cluster_ids.reshape(DEVICES, ROWS_DEV)
    onehot = (blocks[:, :, None] == jnp.arange(CLUSTERS, dtype=jnp.int32)[None, None, :]).astype(jnp.int32)
    member_rank = jnp.sum(jnp.cumsum(onehot, axis=1) * onehot, axis=2) - 1
    position = jnp.arange(DEVICES, dtype=jnp.int32)[:, None] * CAP + member_rank
    flat_index = (blocks * GROUP_SLOTS + position).reshape(-1).astype(jnp.int32)
    row_table = jnp.zeros((CLUSTERS * GROUP_SLOTS,), jnp.int32).at[flat_index].set(jnp.arange(TOTAL, dtype=jnp.int32))
    live_table = jnp.zeros((CLUSTERS * GROUP_SLOTS,), jnp.int32).at[flat_index].set(jnp.ones((TOTAL,), jnp.int32))
    row_table = row_table.reshape(CLUSTERS, GROUP_SLOTS)
    live_table = live_table.reshape(CLUSTERS, GROUP_SLOTS)
    scale = D ** -0.5

    def one_cluster(inputs):
        rows_index, live = inputs
        members = embeddings[rows_index]
        scores = jnp.dot(members, members.T, preferred_element_type=jnp.float32) * scale
        key_mask = (live[None, :] > 0) & jnp.logical_not(jnp.eye(GROUP_SLOTS, dtype=bool))
        shifted = jnp.where(key_mask, scores, prior_score)
        peak = jnp.maximum(jnp.max(shifted, axis=1), prior_score)
        terms = jnp.where(key_mask, jnp.exp(shifted - peak[:, None]), 0.0)
        total = jnp.exp(prior_score - peak) + jnp.sum(terms, axis=1)
        return peak + jnp.log(total)

    dens_table = lax.map(one_cluster, (row_table, live_table))
    return dens_table.reshape(-1)[flat_index]
```

```python
import math

import jax
import jax.numpy as jnp
from jax import lax
from jax.experimental import pallas as pl
from jax.experimental.pallas import tpu as pltpu
from jax.sharding import PartitionSpec as P

prior_score = math.log(64.0)
ABSENT = 32.0
HIDDEN = -1e30
LANES = 128
SLOTS = 8


def iota(shape, dim):
    return lax.broadcasted_iota(jnp.int32, shape, dim)


def whole(shape):
    return pl.BlockSpec(shape, lambda: (0,) * len(shape))


def dot(a, b):
    return jnp.dot(a, b, preferred_element_type=jnp.float32)


def dot_t(a, b):
    return lax.dot_general(a, b, (((1,), (1,)), ((), ())), preferred_element_type=jnp.float32)


def pack_kernel(cluster_ref, rows_ref, send_ref, slot_ref):
    row_count, width = rows_ref.shape
    owners = send_ref.shape[0] // SLOTS
    main = width - LANES
    ids = cluster_ref[...]
    owner = iota((owners, row_count), 0)
    named = owner == ids
    before = (iota((row_count, row_count), 0) < iota((row_count, row_count), 1)).astype(jnp.bfloat16)
    earlier = dot(named.astype(jnp.bfloat16), before)
    rank = jnp.sum(jnp.where(named, earlier, 0.0), axis=0, keepdims=True).astype(jnp.int32)
    slot = ids * SLOTS + rank
    slot_ref[...] = slot
    place = iota((owners * SLOTS, row_count), 0) == slot
    place_f = place.astype(jnp.float32)
    filled = jnp.sum(place_f, axis=1, keepdims=True)
    place_b = place_f.astype(jnp.bfloat16)
    slots = dot(place_b, rows_ref[:, :main])
    lane = iota((owners * SLOTS, LANES), 1)
    level = iota((owners * SLOTS, LANES), 0) % SLOTS
    last = level == SLOTS - 1
    for j in range(main // LANES):
        chunk = slots[:, j * LANES : (j + 1) * LANES]
        if j == 0:
            chunk = jnp.where((lane == 0) & (filled == 0.0), ABSENT, chunk)
        here = (owner * SLOTS + j == slot).astype(jnp.bfloat16)
        rest = dot(here, rows_ref[:, main:])
        rest = jnp.broadcast_to(rest[:, None, :], (owners, SLOTS, LANES)).reshape(owners * SLOTS, LANES)
        chunk = jnp.where(last, rest, chunk)
        send_ref[:, j * LANES : (j + 1) * LANES] = chunk.astype(jnp.bfloat16)


def pack(ids, rows):
    row_count, width = rows.shape
    owners = LANES
    return pl.pallas_call(
        pack_kernel,
        out_shape=(
            jax.ShapeDtypeStruct((owners * SLOTS, width - LANES), jnp.bfloat16),
            jax.ShapeDtypeStruct((1, row_count), jnp.int32),
        ),
        name="pack",
    )(ids, rows)


def full_rows(got_ref, full_ref):
    count, main = got_ref.shape
    levels = main // LANES
    block = LANES
    shape = (block, levels * block)
    r, c = iota(shape, 0), iota(shape, 1)
    pick = ((c % block) == (r // SLOTS) * SLOTS + SLOTS - 1) & ((c // block) == r % SLOTS)
    pick = pick.astype(jnp.bfloat16)
    full_ref[:, :main] = got_ref[...]
    for b in range(count // block):
        rows = got_ref[b * block : (b + 1) * block, :]
        stacked = jnp.concatenate([rows[:, j * LANES : (j + 1) * LANES] for j in range(levels)], axis=0)
        full_ref[b * block : (b + 1) * block, main:] = dot(pick, stacked).astype(jnp.bfloat16)


def key_bias(full_ref):
    count = full_ref.shape[0]
    first = (iota((SLOTS, LANES), 1) == 0).astype(jnp.bfloat16)
    lead = dot_t(first, full_ref[:, :LANES])[:1]
    level = iota((1, count), 1) % SLOTS
    return jnp.where((lead > 0.5 * ABSENT + 8.0) | (level == SLOTS - 1), HIDDEN, 0.0)


TILE = 128


def own_kernel(got_ref, full_ref, peak_ref, total_ref):
    full_rows(got_ref, full_ref)
    count, width = full_ref.shape
    scale = width ** -0.5
    bias = key_bias(full_ref)
    for t in range(count // TILE):
        q = full_ref[t * TILE : (t + 1) * TILE, :]
        scores = dot_t(q, full_ref[...]) * scale + bias
        me = iota(scores.shape, 1) == iota(scores.shape, 0) + t * TILE
        scores = jnp.where(me, HIDDEN, scores)
        peak = jnp.maximum(jnp.max(scores, axis=1, keepdims=True), prior_score)
        total = jnp.exp(prior_score - peak) + jnp.sum(jnp.exp(scores - peak), axis=1, keepdims=True)
        peak_ref[t * TILE : (t + 1) * TILE, :] = peak
        total_ref[t * TILE : (t + 1) * TILE, :] = total


def other_kernel(own_ref, got_ref, peak_ref, total_ref, density_ref, full_ref):
    full_rows(got_ref, full_ref)
    count, width = full_ref.shape
    scale = width ** -0.5
    bias = key_bias(full_ref)
    for t in range(count // TILE):
        q = own_ref[t * TILE : (t + 1) * TILE, :]
        scores = dot_t(q, full_ref[...]) * scale + bias
        before = peak_ref[t * TILE : (t + 1) * TILE, :]
        peak = jnp.maximum(jnp.max(scores, axis=1, keepdims=True), before)
        total = total_ref[t * TILE : (t + 1) * TILE, :] * jnp.exp(before - peak) + jnp.sum(
            jnp.exp(scores - peak), axis=1, keepdims=True
        )
        density = peak + jnp.log(total)
        spread = jnp.where(
            iota((TILE, LANES), 1) == iota((TILE, LANES), 0) % SLOTS, density, 0.0
        ).reshape(TILE // SLOTS, SLOTS, LANES)
        density_ref[t * TILE // SLOTS : (t + 1) * TILE // SLOTS] = jnp.sum(spread, axis=1, keepdims=True)


def pick_kernel(returned_ref, slot_ref, density_ref):
    owners = returned_ref.shape[0]
    values = returned_ref[...].reshape(owners, LANES)
    slot = slot_ref[...]
    count = slot.shape[1]
    named = (iota((owners, count), 0) == slot // SLOTS).astype(jnp.bfloat16)
    turned = values.T[:SLOTS]
    high = turned.astype(jnp.bfloat16)
    left = turned - high.astype(jnp.float32)
    middle = left.astype(jnp.bfloat16)
    low = (left - middle.astype(jnp.float32)).astype(jnp.bfloat16)
    picked = (dot(low, named) + dot(middle, named)) + dot(high, named)
    mine = iota((SLOTS, count), 0) == slot % SLOTS
    density_ref[...] = jnp.sum(jnp.where(mine, picked, 0.0), axis=0, keepdims=True)


def shards(embeddings, cluster):
    owners = lax.axis_size("gx")
    row_count, width = embeddings.shape
    main = width - LANES
    slot_count = owners * SLOTS
    send, slot = pack(cluster.reshape(1, row_count), embeddings)
    got = lax.all_to_all(
        send.reshape(owners, SLOTS, main), "gx", split_axis=0, concat_axis=0, tiled=True
    ).reshape(slot_count, main)
    other = lax.ppermute(got, "gy", [(0, 1), (1, 0)])
    own, peak, total = pl.pallas_call(
        own_kernel,
        out_shape=(
            jax.ShapeDtypeStruct((slot_count, width), jnp.bfloat16),
            jax.ShapeDtypeStruct((slot_count, 1), jnp.float32),
            jax.ShapeDtypeStruct((slot_count, 1), jnp.float32),
        ),
        name="own",
    )(got)
    density = pl.pallas_call(
        other_kernel,
        out_shape=jax.ShapeDtypeStruct((owners, 1, LANES), jnp.float32),
        scratch_shapes=[pltpu.VMEM((slot_count, width), jnp.bfloat16)],
        name="other",
    )(own, other, peak, total)
    returned = lax.all_to_all(density, "gx", split_axis=0, concat_axis=0, tiled=True)
    picked = pl.pallas_call(
        pick_kernel,
        out_shape=jax.ShapeDtypeStruct((1, row_count), jnp.float32),
        name="pick",
    )(returned, slot)
    return picked.reshape(row_count)


def solution(mesh):
    return jax.shard_map(
        shards,
        mesh=mesh,
        in_specs=(P(("gx", "gy"), None), P(("gx", "gy"), None)),
        out_specs=P(("gx", "gy")),
        check_vma=False,
    )
```

```python
import math

import jax
import jax.numpy as jnp
from jax import lax
from jax.experimental import pallas as pl
from jax.experimental.pallas import tpu as pltpu
from jax.sharding import PartitionSpec as P

LOG2E = math.log2(math.e)
LN2 = math.log(2.0)
PRIOR = 6.0
ABSENT = 32.0
HIDDEN = -1e30
LANES = 128
SLOTS = 8
LAST = SLOTS - 1
ROWS = 512
TILE = 64


def iota(shape, dim):
    return lax.broadcasted_iota(jnp.int32, shape, dim)


def dot(a, b):
    return jnp.dot(a, b, preferred_element_type=jnp.float32)


def dot_t(a, b):
    return lax.dot_general(a, b, (((1,), (1,)), ((), ())), preferred_element_type=jnp.float32)


def on_chip(x):
    return pltpu.with_memory_space_constraint(x, pltpu.VMEM)


def chunk_of(j):
    return slice(j * LANES, (j + 1) * LANES)


VMEM_SPEC = pl.BlockSpec(memory_space=pltpu.VMEM)
ANY_SPEC = pl.BlockSpec(memory_space=pl.ANY)
PARAMS = pltpu.CompilerParams(vmem_limit_bytes=16 << 20)


def pack_kernel(cluster_ref, rows_hbm, send_ref, slot_ref, rows_ref, place_ref, sem):
    copy = pltpu.make_async_copy(rows_hbm, rows_ref, sem)
    copy.start()
    row_count, width = rows_ref.shape
    count, main = send_ref.shape
    owners = count // SLOTS
    ids = cluster_ref[...]
    named = iota((owners, row_count), 0) == ids
    before = (iota((row_count, row_count), 0) < iota((row_count, row_count), 1)).astype(jnp.bfloat16)
    earlier = dot(named.astype(jnp.bfloat16), before)
    rank = jnp.sum(jnp.where(named, earlier, 0.0), axis=0, keepdims=True).astype(jnp.int32)
    slot = ids * SLOTS + rank
    slot_ref[...] = slot
    place = (iota((count, row_count), 0) == slot).astype(jnp.float32)
    filled = jnp.sum(place, axis=1, keepdims=True)
    place_ref[...] = place.astype(jnp.bfloat16)
    copy.wait()
    level = iota((owners, SLOTS, LANES), 1)
    rest = None
    for n in reversed(range(width // (2 * LANES))):
        pair = dot(place_ref[...], rows_ref[:, 2 * n * LANES : 2 * (n + 1) * LANES])
        for j in (2 * n, 2 * n + 1):
            chunk = pair[:, (j % 2) * LANES : (j % 2 + 1) * LANES]
            if rest is None:
                rest = pair[:, LANES:].reshape(owners, SLOTS, LANES)
            if j * LANES == main:
                continue
            if j == 0:
                empty = (iota((count, LANES), 1) == 0) & (filled == 0.0)
                chunk = jnp.where(empty, ABSENT, chunk)
            moved = pltpu.roll(rest, (LAST - j) % SLOTS, 1)
            chunk = jnp.where(level == LAST, moved, chunk.reshape(owners, SLOTS, LANES))
            send_ref[:, chunk_of(j)] = chunk.reshape(count, LANES).astype(jnp.bfloat16)


def full_rows(got_ref, full_ref):
    count, main = got_ref.shape
    shape = (count // SLOTS, SLOTS, LANES)
    level = iota(shape, 1)
    full_ref[:, :main] = got_ref[...]
    rest = jnp.zeros(shape, jnp.float32)
    for j in range(main // LANES):
        chunk = got_ref[:, chunk_of(j)].astype(jnp.float32).reshape(shape)
        rest = jnp.where(level == j, pltpu.roll(chunk, (j - LAST) % SLOTS, 1), rest)
    full_ref[:, main:] = rest.reshape(count, LANES).astype(jnp.bfloat16)


def key_bias(full_ref):
    count = full_ref.shape[0]
    first = (iota((SLOTS, LANES), 1) == 0).astype(jnp.bfloat16)
    lead = dot_t(first, full_ref[:, :LANES])[:1]
    level = iota((1, count), 1) % SLOTS
    return jnp.where((lead > 0.75 * ABSENT) | (level == LAST), HIDDEN, 0.0)


def score_rows(query_ref, key_ref, bias, scores_ref, m, own):
    count, width = key_ref.shape
    wide = 2 * LANES
    first = m * ROWS
    for n in range(count // wide):
        scores = dot_t(query_ref[first : first + ROWS, :], key_ref[n * wide : (n + 1) * wide, :])
        scores = scores * (LOG2E * width**-0.5) + bias[:, n * wide : (n + 1) * wide]
        if own and first <= n * wide < first + ROWS:
            me = iota(scores.shape, 1) + (n * wide - first) == iota(scores.shape, 0)
            scores = jnp.where(me, HIDDEN, scores)
        scores_ref[first : first + ROWS, n * wide : (n + 1) * wide] = scores


def own_kernel(got_ref, full_ref, peak_ref, total_ref, scores_ref):
    full_rows(got_ref, full_ref)
    bias = key_bias(full_ref)
    for m in range(full_ref.shape[0] // ROWS):
        score_rows(full_ref, full_ref, bias, scores_ref, m, True)
        for t in range(m * ROWS, (m + 1) * ROWS, TILE):
            scores = scores_ref[t : t + TILE, :]
            peak = jnp.maximum(jnp.max(scores, axis=1, keepdims=True), PRIOR)
            total = jnp.exp2(PRIOR - peak) + jnp.sum(jnp.exp2(scores - peak), axis=1, keepdims=True)
            peak_ref[t : t + TILE, :] = peak
            total_ref[t : t + TILE, :] = total


def other_kernel(own_ref, got_ref, peak_ref, total_ref, density_ref, full_ref, scores_ref):
    full_rows(got_ref, full_ref)
    bias = key_bias(full_ref)
    for m in range(full_ref.shape[0] // ROWS):
        score_rows(own_ref, full_ref, bias, scores_ref, m, False)
        for t in range(m * ROWS, (m + 1) * ROWS, TILE):
            scores = scores_ref[t : t + TILE, :]
            before = peak_ref[t : t + TILE, :]
            peak = jnp.maximum(jnp.max(scores, axis=1, keepdims=True), before)
            total = total_ref[t : t + TILE, :] * jnp.exp2(before - peak) + jnp.sum(
                jnp.exp2(scores - peak), axis=1, keepdims=True
            )
            density = peak * LN2 + jnp.log(total)
            mine = iota((TILE, LANES), 1) == iota((TILE, LANES), 0) % SLOTS
            spread = jnp.where(mine, density, 0.0).reshape(TILE // SLOTS, SLOTS, LANES)
            density_ref[t // SLOTS : (t + TILE) // SLOTS] = jnp.sum(spread, axis=1, keepdims=True)


def pick_kernel(returned_ref, slot_ref, density_ref):
    owners = returned_ref.shape[0]
    values = returned_ref[...].reshape(owners, LANES)
    slot = slot_ref[...]
    count = slot.shape[1]
    named = (iota((owners, count), 0) == slot // SLOTS).astype(jnp.bfloat16)
    turned = values.T[:SLOTS]
    high = turned.astype(jnp.bfloat16)
    left = turned - high.astype(jnp.float32)
    middle = left.astype(jnp.bfloat16)
    low = (left - middle.astype(jnp.float32)).astype(jnp.bfloat16)
    picked = (dot(low, named) + dot(middle, named)) + dot(high, named)
    mine = iota((SLOTS, count), 0) == slot % SLOTS
    density_ref[...] = jnp.sum(jnp.where(mine, picked, 0.0), axis=0, keepdims=True)


def shards(embeddings, cluster):
    owners = lax.axis_size("gx")
    row_count, width = embeddings.shape
    main = width - LANES
    slot_count = owners * SLOTS
    send, slot = pl.pallas_call(
        pack_kernel,
        in_specs=[VMEM_SPEC, ANY_SPEC],
        out_shape=(
            jax.ShapeDtypeStruct((slot_count, main), jnp.bfloat16),
            pltpu.VMEM((1, row_count), jnp.int32),
        ),
        scratch_shapes=[
            pltpu.VMEM((row_count, width), jnp.bfloat16),
            pltpu.VMEM((slot_count, row_count), jnp.bfloat16),
            pltpu.SemaphoreType.DMA,
        ],
        compiler_params=PARAMS,
        name="pack",
    )(
        cluster.reshape(1, row_count),
        pltpu.with_memory_space_constraint(embeddings, pltpu.HBM),
    )
    got = lax.all_to_all(
        send.reshape(owners, SLOTS, main), "gx", split_axis=0, concat_axis=0, tiled=True
    ).reshape(slot_count, main)
    other = lax.ppermute(got, "gy", [(0, 1), (1, 0)])
    own, peak, total = pl.pallas_call(
        own_kernel,
        in_specs=[VMEM_SPEC],
        out_shape=(
            pltpu.VMEM((slot_count, width), jnp.bfloat16),
            pltpu.VMEM((slot_count, 1), jnp.float32),
            pltpu.VMEM((slot_count, 1), jnp.float32),
        ),
        scratch_shapes=[pltpu.VMEM((slot_count, slot_count), jnp.float32)],
        compiler_params=PARAMS,
        name="own",
    )(on_chip(got))
    density = pl.pallas_call(
        other_kernel,
        in_specs=[VMEM_SPEC] * 4,
        out_shape=jax.ShapeDtypeStruct((owners, 1, LANES), jnp.float32),
        scratch_shapes=[
            pltpu.VMEM((slot_count, width), jnp.bfloat16),
            pltpu.VMEM((slot_count, slot_count), jnp.float32),
        ],
        compiler_params=PARAMS,
        name="other",
    )(on_chip(own), on_chip(other), on_chip(peak), on_chip(total))
    returned = lax.all_to_all(density, "gx", split_axis=0, concat_axis=0, tiled=True)
    picked = pl.pallas_call(
        pick_kernel,
        in_specs=[VMEM_SPEC, VMEM_SPEC],
        out_shape=jax.ShapeDtypeStruct((1, row_count), jnp.float32),
        compiler_params=PARAMS,
        name="pick",
    )(on_chip(returned), on_chip(slot))
    return picked.reshape(row_count)


def solution(mesh):
    return jax.shard_map(
        shards,
        mesh=mesh,
        in_specs=(P(("gx", "gy"), None), P(("gx", "gy"), None)),
        out_specs=P(("gx", "gy")),
        check_vma=False,
    )
```

```python
import math

import jax
import jax.numpy as jnp
from jax import lax
from jax.experimental import pallas as pl
from jax.experimental.pallas import tpu as pltpu
from jax.sharding import PartitionSpec as P

LOG2E = math.log2(math.e)
LN2 = math.log(2.0)
PRIOR = 6.0
ABSENT = 32.0
HIDDEN = -1e30
LANES = 128
SLOTS = 8
LAST = SLOTS - 1
SHARED = LANES // SLOTS
BLOCK = 512
PART = 512
COPIES = 4


def iota(shape, dim):
    return lax.broadcasted_iota(jnp.int32, shape, dim)


def dot(a, b):
    return jnp.dot(a, b, preferred_element_type=jnp.float32)


def dot_t(a, b):
    return lax.dot_general(a, b, (((1,), (1,)), ((), ())), preferred_element_type=jnp.float32)


def on_chip(x):
    return pltpu.with_memory_space_constraint(x, pltpu.VMEM)


def chunk_of(j):
    return slice(j * LANES, (j + 1) * LANES)


VMEM_SPEC = pl.BlockSpec(memory_space=pltpu.VMEM)
ANY_SPEC = pl.BlockSpec(memory_space=pl.ANY)
PARAMS = pltpu.CompilerParams(vmem_limit_bytes=16 << 20)


def pack_kernel(cluster_hbm, rows_hbm, send_ref, slot_ref, cluster_ref, rows_ref, place_ref, sems):
    row_count, width = rows_ref.shape
    part = row_count // COPIES
    ids_copy = pltpu.make_async_copy(cluster_hbm, cluster_ref, sems.at[COPIES])
    ids_copy.start()
    copies = []
    for n in range(COPIES):
        some = slice(n * part, (n + 1) * part)
        copies.append(pltpu.make_async_copy(rows_hbm.at[some, :], rows_ref.at[some, :], sems.at[n]))
        copies[n].start()
    count, main = send_ref.shape
    owners = count // SLOTS
    before = (iota((row_count, row_count), 0) < iota((row_count, row_count), 1)).astype(jnp.bfloat16)
    ids_copy.wait()
    ids = cluster_ref[...]
    named = iota((owners, row_count), 0) == ids
    earlier = dot(named.astype(jnp.bfloat16), before)
    rank = jnp.sum(jnp.where(named, earlier, 0.0), axis=0, keepdims=True).astype(jnp.int32)
    slot = ids * SLOTS + rank
    slot_ref[...] = slot
    place = (iota((count, row_count), 0) == slot).astype(jnp.float32)
    filled = jnp.sum(place, axis=1, keepdims=True)
    place_ref[...] = place.astype(jnp.bfloat16)
    level = iota((owners, SLOTS, LANES), 1)
    rest = None
    for copy in copies:
        copy.wait()
    for n in reversed(range(width // (2 * LANES))):
        pair = dot(place_ref[...], rows_ref[:, 2 * n * LANES : 2 * (n + 1) * LANES])
        for j in (2 * n, 2 * n + 1):
            chunk = pair[:, (j % 2) * LANES : (j % 2 + 1) * LANES]
            if rest is None:
                rest = pair[:, LANES:].reshape(owners, SLOTS, LANES)
            if j * LANES == main:
                continue
            if j == 0:
                empty = (iota((count, LANES), 1) == 0) & (filled == 0.0)
                chunk = jnp.where(empty, ABSENT, chunk)
            moved = pltpu.roll(rest, (LAST - j) % SLOTS, 1)
            chunk = jnp.where(level == LAST, moved, chunk.reshape(owners, SLOTS, LANES))
            send_ref[:, chunk_of(j)] = chunk.reshape(count, LANES).astype(jnp.bfloat16)


def full_rows(got_ref, full_ref):
    count, main = got_ref.shape
    shape = (count // SLOTS, SLOTS, LANES)
    level = iota(shape, 1)
    full_ref[:, :main] = got_ref[...]
    rest = jnp.zeros(shape, jnp.float32)
    for j in range(main // LANES):
        chunk = got_ref[:, chunk_of(j)].astype(jnp.float32).reshape(shape)
        rest = jnp.where(level == j, pltpu.roll(chunk, (j - LAST) % SLOTS, 1), rest)
    full_ref[:, main:] = rest.reshape(count, LANES).astype(jnp.bfloat16)


def hide_keys(full_ref, bias_ref):
    count = full_ref.shape[0]
    lead = full_ref[:, :LANES].astype(jnp.float32)[:, :1]
    level = iota((count, LANES), 0) % SLOTS
    bias_ref[...] = jnp.where((lead > 0.75 * ABSENT) | (level == LAST), HIDDEN, 0.0)


def score_part(key_ref, query_ref, bias_ref, scores_ref, n, part, own):
    width = key_ref.shape[1]
    keys = slice(part * PART, (part + 1) * PART)
    scores = dot_t(key_ref[keys, :], query_ref[n * BLOCK : (n + 1) * BLOCK, :])
    bias = jnp.concatenate([bias_ref[keys, :]] * (BLOCK // LANES), axis=1)
    scores = scores * (LOG2E * width**-0.5) + bias
    if own and part * PART <= n * BLOCK < (part + 1) * PART:
        me = iota(scores.shape, 0) == iota(scores.shape, 1) + (n * BLOCK - part * PART)
        scores = jnp.where(me, HIDDEN, scores)
    scores_ref[n, keys, :] = scores
    return jnp.max(scores, axis=0, keepdims=True)


def fold(key_ref, query_ref, bias_ref, scores_ref, own, before, finish):
    count = key_ref.shape[0]
    blocks, parts = count // BLOCK, count // PART
    peaks, totals = {}, {}
    for n in range(blocks + 1):
        if n < blocks:
            peaks[n], totals[n] = before(n)
            old, new = peaks[n], peaks[n]
        for part in range(parts):
            if n < blocks:
                new = jnp.maximum(
                    new, score_part(key_ref, query_ref, bias_ref, scores_ref, n, part, own)
                )
            if n > 0:
                scores = scores_ref[n - 1, part * PART : (part + 1) * PART, :]
                totals[n - 1] += jnp.sum(jnp.exp2(scores - peaks[n - 1]), axis=0, keepdims=True)
        if n < blocks:
            totals[n] = totals[n] * jnp.exp2(old - new)
            peaks[n] = new
        if n > 0:
            finish(n - 1, peaks[n - 1], totals[n - 1])


def own_kernel(got_ref, full_ref, peak_ref, total_ref, bias_ref, scores_ref):
    full_rows(got_ref, full_ref)
    hide_keys(full_ref, bias_ref)

    def before(n):
        return jnp.full((1, BLOCK), PRIOR, jnp.float32), jnp.ones((1, BLOCK), jnp.float32)

    def finish(n, peak, total):
        peak_ref[:, n * BLOCK : (n + 1) * BLOCK] = peak
        total_ref[:, n * BLOCK : (n + 1) * BLOCK] = total

    fold(full_ref, full_ref, bias_ref, scores_ref, True, before, finish)


def other_kernel(own_ref, got_ref, peak_ref, total_ref, density_ref, full_ref, bias_ref, scores_ref):
    full_rows(got_ref, full_ref)
    hide_keys(full_ref, bias_ref)

    def before(n):
        lanes = slice(n * BLOCK, (n + 1) * BLOCK)
        return peak_ref[:, lanes], total_ref[:, lanes]

    def finish(n, peak, total):
        density = peak * LN2 + jnp.log(total)
        for v in range(BLOCK // LANES):
            row = density[:, chunk_of(v)].reshape(1, 1, LANES)
            first = (n * BLOCK + v * LANES) // SLOTS
            density_ref[first : first + SHARED] = jnp.broadcast_to(row, (SHARED, 1, LANES))

    fold(full_ref, own_ref, bias_ref, scores_ref, False, before, finish)


def pick_kernel(returned_ref, slot_ref, density_ref):
    owners = returned_ref.shape[0]
    values = returned_ref[...].reshape(owners, LANES)
    slot = slot_ref[...]
    count = slot.shape[1]
    named = (iota((owners, count), 0) == slot // SLOTS).astype(jnp.bfloat16)
    turned = values.T
    high = turned.astype(jnp.bfloat16)
    left = turned - high.astype(jnp.float32)
    middle = left.astype(jnp.bfloat16)
    low = (left - middle.astype(jnp.float32)).astype(jnp.bfloat16)
    picked = (dot(low, named) + dot(middle, named)) + dot(high, named)
    lane = slot % SLOTS + (lax.axis_index("gx") % SHARED) * SLOTS
    mine = iota((LANES, count), 0) == lane
    density_ref[...] = jnp.sum(jnp.where(mine, picked, 0.0), axis=0, keepdims=True)


def shards(embeddings, cluster):
    owners = lax.axis_size("gx")
    row_count, width = embeddings.shape
    main = width - LANES
    slot_count = owners * SLOTS
    send, slot = pl.pallas_call(
        pack_kernel,
        in_specs=[ANY_SPEC, ANY_SPEC],
        out_shape=(
            jax.ShapeDtypeStruct((slot_count, main), jnp.bfloat16),
            pltpu.VMEM((1, row_count), jnp.int32),
        ),
        scratch_shapes=[
            pltpu.VMEM((1, row_count), jnp.int32),
            pltpu.VMEM((row_count, width), jnp.bfloat16),
            pltpu.VMEM((slot_count, row_count), jnp.bfloat16),
            pltpu.SemaphoreType.DMA((COPIES + 1,)),
        ],
        compiler_params=PARAMS,
        name="pack",
    )(
        pltpu.with_memory_space_constraint(cluster.reshape(1, row_count), pltpu.HBM),
        pltpu.with_memory_space_constraint(embeddings, pltpu.HBM),
    )
    got = lax.all_to_all(
        send.reshape(owners, SLOTS, main), "gx", split_axis=0, concat_axis=0, tiled=True
    ).reshape(slot_count, main)
    other = lax.ppermute(got, "gy", [(0, 1), (1, 0)])
    own, peak, total = pl.pallas_call(
        own_kernel,
        in_specs=[VMEM_SPEC],
        out_shape=(
            pltpu.VMEM((slot_count, width), jnp.bfloat16),
            pltpu.VMEM((1, slot_count), jnp.float32),
            pltpu.VMEM((1, slot_count), jnp.float32),
        ),
        scratch_shapes=[
            pltpu.VMEM((slot_count, LANES), jnp.float32),
            pltpu.VMEM((slot_count // BLOCK, slot_count, BLOCK), jnp.float32),
        ],
        compiler_params=PARAMS,
        name="own",
    )(on_chip(got))
    density = pl.pallas_call(
        other_kernel,
        in_specs=[VMEM_SPEC] * 4,
        out_shape=jax.ShapeDtypeStruct((owners, 1, LANES), jnp.float32),
        scratch_shapes=[
            pltpu.VMEM((slot_count, width), jnp.bfloat16),
            pltpu.VMEM((slot_count, LANES), jnp.float32),
            pltpu.VMEM((slot_count // BLOCK, slot_count, BLOCK), jnp.float32),
        ],
        compiler_params=PARAMS,
        name="other",
    )(on_chip(own), on_chip(other), on_chip(peak), on_chip(total))
    returned = lax.all_to_all(density, "gx", split_axis=0, concat_axis=0, tiled=True)
    picked = pl.pallas_call(
        pick_kernel,
        in_specs=[VMEM_SPEC, VMEM_SPEC],
        out_shape=jax.ShapeDtypeStruct((1, row_count), jnp.float32),
        compiler_params=PARAMS,
        name="pick",
    )(on_chip(returned), on_chip(slot))
    return picked.reshape(row_count)


def solution(mesh):
    return jax.shard_map(
        shards,
        mesh=mesh,
        in_specs=(P(("gx", "gy"), None), P(("gx", "gy"), None)),
        out_specs=P(("gx", "gy")),
        check_vma=False,
    )
```

```python
import math

import jax
import jax.numpy as jnp
from jax import lax
from jax.experimental import pallas as pl
from jax.experimental.pallas import tpu as pltpu
from jax.sharding import PartitionSpec as P

LOG2E = math.log2(math.e)
LN2 = math.log(2.0)
PRIOR = 6.0
ABSENT = 32.0
HIDDEN = -1e30
LANES = 128
SLOTS = 8
LAST = SLOTS - 1
SHARED = LANES // SLOTS
BLOCK = 512
PART = 512
COPIES = 4


def iota(shape, dim):
    return lax.broadcasted_iota(jnp.int32, shape, dim)


def dot(a, b):
    return jnp.dot(a, b, preferred_element_type=jnp.float32)


def dot_t(a, b):
    return lax.dot_general(a, b, (((1,), (1,)), ((), ())), preferred_element_type=jnp.float32)


def on_chip(x):
    return pltpu.with_memory_space_constraint(x, pltpu.VMEM)


def chunk_of(j):
    return slice(j * LANES, (j + 1) * LANES)


VMEM_SPEC = pl.BlockSpec(memory_space=pltpu.VMEM)
ANY_SPEC = pl.BlockSpec(memory_space=pl.ANY)
PARAMS = pltpu.CompilerParams(vmem_limit_bytes=16 << 20)


def pack_kernel(cluster_hbm, rows_hbm, send_ref, slot_ref, cluster_ref, rows_ref, place_ref, sems):
    row_count, width = rows_ref.shape
    part = row_count // COPIES
    ids_copy = pltpu.make_async_copy(cluster_hbm, cluster_ref, sems.at[COPIES])
    ids_copy.start()
    copies = []
    for n in range(COPIES):
        some = slice(n * part, (n + 1) * part)
        copies.append(pltpu.make_async_copy(rows_hbm.at[some, :], rows_ref.at[some, :], sems.at[n]))
        copies[n].start()
    count, main = send_ref.shape
    owners = count // SLOTS
    before = (iota((row_count, row_count), 0) < iota((row_count, row_count), 1)).astype(jnp.bfloat16)
    ids_copy.wait()
    ids = cluster_ref[...]
    named = iota((owners, row_count), 0) == ids
    earlier = dot(named.astype(jnp.bfloat16), before)
    rank = jnp.sum(jnp.where(named, earlier, 0.0), axis=0, keepdims=True).astype(jnp.int32)
    slot = ids * SLOTS + rank
    slot_ref[...] = slot
    some = 2 * SLOTS
    ahead = jnp.broadcast_to(slot, (some, row_count)) - iota((some, row_count), 0)
    ahead = ahead.astype(jnp.int16)
    for i in range(count // some):
        place_ref[i * some : (i + 1) * some, :] = jnp.where(
            ahead == i * some, jnp.ones((), jnp.bfloat16), jnp.zeros((), jnp.bfloat16)
        )
    members = jnp.sum(named.astype(jnp.float32), axis=1, keepdims=True)
    members = jnp.broadcast_to(members, (owners, LANES))[:, None, :]
    level = iota((owners, SLOTS, LANES), 1)
    rest = None
    for copy in copies:
        copy.wait()
    for n in reversed(range(width // (2 * LANES))):
        pair = dot(place_ref[...], rows_ref[:, 2 * n * LANES : 2 * (n + 1) * LANES])
        for j in (2 * n, 2 * n + 1):
            chunk = pair[:, (j % 2) * LANES : (j % 2 + 1) * LANES]
            if rest is None:
                rest = pair[:, LANES:].reshape(owners, SLOTS, LANES)
            if j * LANES == main:
                continue
            chunk = chunk.reshape(level.shape)
            if j == 0:
                empty = level.astype(jnp.float32) >= jnp.broadcast_to(members, level.shape)
                chunk = jnp.where(empty & (iota(level.shape, 2) == 0), ABSENT, chunk)
            chunk = jnp.where(level == LAST, pltpu.roll(rest, (LAST - j) % SLOTS, 1), chunk)
            send_ref[:, chunk_of(j)] = chunk.reshape(count, LANES).astype(jnp.bfloat16)


def full_rows(got_ref, full_ref):
    count, main = got_ref.shape
    shape = (count // SLOTS, SLOTS, LANES)
    level = iota(shape, 1)
    full_ref[:, :main] = got_ref[...]
    rest = jnp.zeros(shape, jnp.float32)
    for j in range(main // LANES):
        chunk = got_ref[:, chunk_of(j)].astype(jnp.float32).reshape(shape)
        rest = jnp.where(level == j, pltpu.roll(chunk, (j - LAST) % SLOTS, 1), rest)
    full_ref[:, main:] = rest.reshape(count, LANES).astype(jnp.bfloat16)


def hide_keys(full_ref, bias_ref):
    count = full_ref.shape[0]
    lead = full_ref[:, :LANES].astype(jnp.float32)[:, :1]
    level = iota((count, LANES), 0) % SLOTS
    bias_ref[...] = jnp.where((lead > 0.75 * ABSENT) | (level == LAST), HIDDEN, 0.0)


def score_part(key_ref, query_ref, bias_ref, scores_ref, n, part, own):
    width = key_ref.shape[1]
    keys = slice(part * PART, (part + 1) * PART)
    scores = dot_t(key_ref[keys, :], query_ref[n * BLOCK : (n + 1) * BLOCK, :])
    bias = jnp.concatenate([bias_ref[keys, :]] * (BLOCK // LANES), axis=1)
    scores = scores * (LOG2E * width**-0.5) + bias
    if own and part * PART <= n * BLOCK < (part + 1) * PART:
        me = iota(scores.shape, 0) == iota(scores.shape, 1) + (n * BLOCK - part * PART)
        scores = jnp.where(me, HIDDEN, scores)
    scores_ref[n, keys, :] = scores
    return jnp.max(scores, axis=0, keepdims=True)


def fold(key_ref, query_ref, bias_ref, scores_ref, own, before, finish):
    count = key_ref.shape[0]
    blocks, parts = count // BLOCK, count // PART
    peaks, totals = {}, {}
    for n in range(blocks + 1):
        if n < blocks:
            peaks[n], totals[n] = before(n)
            old, new = peaks[n], peaks[n]
        for part in range(parts):
            if n < blocks:
                new = jnp.maximum(
                    new, score_part(key_ref, query_ref, bias_ref, scores_ref, n, part, own)
                )
            if n > 0:
                scores = scores_ref[n - 1, part * PART : (part + 1) * PART, :]
                totals[n - 1] += jnp.sum(jnp.exp2(scores - peaks[n - 1]), axis=0, keepdims=True)
        if n < blocks:
            totals[n] = totals[n] * jnp.exp2(old - new)
            peaks[n] = new
        if n > 0:
            finish(n - 1, peaks[n - 1], totals[n - 1])


def own_kernel(got_ref, full_ref, peak_ref, total_ref, bias_ref, scores_ref):
    full_rows(got_ref, full_ref)
    hide_keys(full_ref, bias_ref)

    def before(n):
        return jnp.full((1, BLOCK), PRIOR, jnp.float32), jnp.ones((1, BLOCK), jnp.float32)

    def finish(n, peak, total):
        peak_ref[:, n * BLOCK : (n + 1) * BLOCK] = peak
        total_ref[:, n * BLOCK : (n + 1) * BLOCK] = total

    fold(full_ref, full_ref, bias_ref, scores_ref, True, before, finish)


def other_kernel(own_ref, got_ref, peak_ref, total_ref, density_ref, full_ref, bias_ref, scores_ref):
    full_rows(got_ref, full_ref)
    hide_keys(full_ref, bias_ref)

    def before(n):
        lanes = slice(n * BLOCK, (n + 1) * BLOCK)
        return peak_ref[:, lanes], total_ref[:, lanes]

    def finish(n, peak, total):
        density = peak * LN2 + jnp.log(total)
        for v in range(BLOCK // LANES):
            row = density[:, chunk_of(v)].reshape(1, 1, LANES)
            first = (n * BLOCK + v * LANES) // SLOTS
            density_ref[first : first + SHARED] = jnp.broadcast_to(row, (SHARED, 1, LANES))

    fold(full_ref, own_ref, bias_ref, scores_ref, False, before, finish)


def pick_kernel(returned_ref, slot_ref, density_ref):
    owners = returned_ref.shape[0]
    values = returned_ref[...].reshape(owners, LANES)
    slot = slot_ref[...]
    count = slot.shape[1]
    named = (iota((owners, count), 0) == slot // SLOTS).astype(jnp.bfloat16)
    turn = (SHARED - lax.axis_index("gx") % SHARED) % SHARED * SLOTS
    turned = pltpu.roll(values, turn, 1).T[:SLOTS]
    high = turned.astype(jnp.bfloat16)
    left = turned - high.astype(jnp.float32)
    middle = left.astype(jnp.bfloat16)
    low = (left - middle.astype(jnp.float32)).astype(jnp.bfloat16)
    picked = (dot(low, named) + dot(middle, named)) + dot(high, named)
    mine = iota((SLOTS, count), 0) == slot % SLOTS
    density_ref[...] = jnp.sum(jnp.where(mine, picked, 0.0), axis=0, keepdims=True)


def shards(embeddings, cluster):
    owners = lax.axis_size("gx")
    row_count, width = embeddings.shape
    main = width - LANES
    slot_count = owners * SLOTS
    send, slot = pl.pallas_call(
        pack_kernel,
        in_specs=[ANY_SPEC, ANY_SPEC],
        out_shape=(
            jax.ShapeDtypeStruct((slot_count, main), jnp.bfloat16),
            pltpu.VMEM((1, row_count), jnp.int32),
        ),
        scratch_shapes=[
            pltpu.VMEM((1, row_count), jnp.int32),
            pltpu.VMEM((row_count, width), jnp.bfloat16),
            pltpu.VMEM((slot_count, row_count), jnp.bfloat16),
            pltpu.SemaphoreType.DMA((COPIES + 1,)),
        ],
        compiler_params=PARAMS,
        name="pack",
    )(
        pltpu.with_memory_space_constraint(cluster.reshape(1, row_count), pltpu.HBM),
        pltpu.with_memory_space_constraint(embeddings, pltpu.HBM),
    )
    got = lax.all_to_all(
        send.reshape(owners, SLOTS, main), "gx", split_axis=0, concat_axis=0, tiled=True
    ).reshape(slot_count, main)
    other = lax.ppermute(got, "gy", [(0, 1), (1, 0)])
    own, peak, total = pl.pallas_call(
        own_kernel,
        in_specs=[VMEM_SPEC],
        out_shape=(
            pltpu.VMEM((slot_count, width), jnp.bfloat16),
            pltpu.VMEM((1, slot_count), jnp.float32),
            pltpu.VMEM((1, slot_count), jnp.float32),
        ),
        scratch_shapes=[
            pltpu.VMEM((slot_count, LANES), jnp.float32),
            pltpu.VMEM((slot_count // BLOCK, slot_count, BLOCK), jnp.float32),
        ],
        compiler_params=PARAMS,
        name="own",
    )(on_chip(got))
    density = pl.pallas_call(
        other_kernel,
        in_specs=[VMEM_SPEC] * 4,
        out_shape=jax.ShapeDtypeStruct((owners, 1, LANES), jnp.float32),
        scratch_shapes=[
            pltpu.VMEM((slot_count, width), jnp.bfloat16),
            pltpu.VMEM((slot_count, LANES), jnp.float32),
            pltpu.VMEM((slot_count // BLOCK, slot_count, BLOCK), jnp.float32),
        ],
        compiler_params=PARAMS,
        name="other",
    )(on_chip(own), on_chip(other), on_chip(peak), on_chip(total))
    returned = lax.all_to_all(density, "gx", split_axis=0, concat_axis=0, tiled=True)
    picked = pl.pallas_call(
        pick_kernel,
        in_specs=[VMEM_SPEC, VMEM_SPEC],
        out_shape=jax.ShapeDtypeStruct((1, row_count), jnp.float32),
        compiler_params=PARAMS,
        name="pick",
    )(on_chip(returned), on_chip(slot))
    return picked.reshape(row_count)


def solution(mesh):
    return jax.shard_map(
        shards,
        mesh=mesh,
        in_specs=(P(("gx", "gy"), None), P(("gx", "gy"), None)),
        out_specs=P(("gx", "gy")),
        check_vma=False,
    )
```

```python
import math

import jax
import jax.numpy as jnp
from jax import lax
from jax.experimental import pallas as pl
from jax.experimental.pallas import tpu as pltpu
from jax.sharding import PartitionSpec as P

LOG2E = math.log2(math.e)
LN2 = math.log(2.0)
PRIOR = 6.0
ABSENT = 32.0
HIDDEN = -1e30
LANES = 128
SLOTS = 8
LAST = SLOTS - 1
SHARED = LANES // SLOTS
BLOCK = 512
PART = 512
COPIES = 1


def iota(shape, dim):
    return lax.broadcasted_iota(jnp.int32, shape, dim)


def dot(a, b):
    return jnp.dot(a, b, preferred_element_type=jnp.float32)


def dot_t(a, b):
    return lax.dot_general(a, b, (((1,), (1,)), ((), ())), preferred_element_type=jnp.float32)


def on_chip(x):
    return pltpu.with_memory_space_constraint(x, pltpu.VMEM)


def chunk_of(j):
    return slice(j * LANES, (j + 1) * LANES)


VMEM_SPEC = pl.BlockSpec(memory_space=pltpu.VMEM)
ANY_SPEC = pl.BlockSpec(memory_space=pl.ANY)
PARAMS = pltpu.CompilerParams(vmem_limit_bytes=16 << 20)


def pack_kernel(cluster_hbm, rows_hbm, send_ref, slot_ref, cluster_ref, rows_ref, place_ref, sems):
    row_count, width = rows_ref.shape
    part = row_count // COPIES
    ids_copy = pltpu.make_async_copy(cluster_hbm, cluster_ref, sems.at[COPIES])
    ids_copy.start()
    copies = []
    for n in range(COPIES):
        some = slice(n * part, (n + 1) * part)
        copies.append(pltpu.make_async_copy(rows_hbm.at[some, :], rows_ref.at[some, :], sems.at[n]))
        copies[n].start()
    count, main = send_ref.shape
    owners = count // SLOTS
    before = (iota((row_count, row_count), 0) < iota((row_count, row_count), 1)).astype(jnp.bfloat16)
    ids_copy.wait()
    ids = cluster_ref[...]
    named = iota((owners, row_count), 0) == ids
    earlier = dot(named.astype(jnp.bfloat16), before)
    rank = jnp.sum(jnp.where(named, earlier, 0.0), axis=0, keepdims=True).astype(jnp.int32)
    slot = ids * SLOTS + rank
    slot_ref[...] = slot
    some = 2 * SLOTS
    ahead = jnp.broadcast_to(slot, (some, row_count)) - iota((some, row_count), 0)
    ahead = ahead.astype(jnp.int16)
    for i in range(count // some):
        place_ref[i * some : (i + 1) * some, :] = jnp.where(
            ahead == i * some, jnp.ones((), jnp.bfloat16), jnp.zeros((), jnp.bfloat16)
        )
    members = jnp.sum(named.astype(jnp.float32), axis=1, keepdims=True)
    members = jnp.broadcast_to(members, (owners, LANES))[:, None, :]
    level = iota((owners, SLOTS, LANES), 1)
    rest = None
    for copy in copies:
        copy.wait()
    for n in reversed(range(width // (2 * LANES))):
        pair = dot(place_ref[...], rows_ref[:, 2 * n * LANES : 2 * (n + 1) * LANES])
        for j in (2 * n, 2 * n + 1):
            chunk = pair[:, (j % 2) * LANES : (j % 2 + 1) * LANES]
            if rest is None:
                rest = pair[:, LANES:].reshape(owners, SLOTS, LANES)
            if j * LANES == main:
                continue
            chunk = chunk.reshape(level.shape)
            if j == 0:
                empty = level.astype(jnp.float32) >= jnp.broadcast_to(members, level.shape)
                chunk = jnp.where(empty & (iota(level.shape, 2) == 0), ABSENT, chunk)
            chunk = jnp.where(level == LAST, pltpu.roll(rest, (LAST - j) % SLOTS, 1), chunk)
            send_ref[:, chunk_of(j)] = chunk.reshape(count, LANES).astype(jnp.bfloat16)


def full_rows(got_ref, full_ref):
    count, main = got_ref.shape
    shape = (count // SLOTS, SLOTS, LANES)
    level = iota(shape, 1)
    full_ref[:, :main] = got_ref[...]
    rest = jnp.zeros(shape, jnp.float32)
    for j in range(main // LANES):
        chunk = got_ref[:, chunk_of(j)].astype(jnp.float32).reshape(shape)
        rest = jnp.where(level == j, pltpu.roll(chunk, (j - LAST) % SLOTS, 1), rest)
    full_ref[:, main:] = rest.reshape(count, LANES).astype(jnp.bfloat16)


def hide_keys(full_ref, bias_ref):
    count = full_ref.shape[0]
    lead = full_ref[:, :LANES].astype(jnp.float32)[:, :1]
    level = iota((count, LANES), 0) % SLOTS
    bias_ref[...] = jnp.where((lead > 0.75 * ABSENT) | (level == LAST), HIDDEN, 0.0)


def score_part(key_ref, query_ref, bias_ref, scores_ref, n, part, own):
    width = key_ref.shape[1]
    keys = slice(part * PART, (part + 1) * PART)
    lanes = slice(n * BLOCK, (n + 1) * BLOCK)
    if own:
        scores = dot_t(key_ref[keys, :], query_ref[lanes, :])
    else:
        scores = dot(key_ref[keys, :], query_ref[:, lanes])
    bias = jnp.concatenate([bias_ref[keys, :]] * (BLOCK // LANES), axis=1)
    scores = scores * (LOG2E * width**-0.5) + bias
    if own and part * PART <= n * BLOCK < (part + 1) * PART:
        me = iota(scores.shape, 0) == iota(scores.shape, 1) + (n * BLOCK - part * PART)
        scores = jnp.where(me, HIDDEN, scores)
    scores_ref[n, keys, :] = scores
    return jnp.max(scores, axis=0, keepdims=True)


def fold(key_ref, query_ref, bias_ref, scores_ref, own, before, finish):
    count = key_ref.shape[0]
    blocks, parts = count // BLOCK, count // PART
    peaks, totals = {}, {}
    for n in range(blocks + 1):
        if n < blocks:
            peaks[n], totals[n] = before(n)
            old, new = peaks[n], peaks[n]
        for part in range(parts):
            if n < blocks:
                new = jnp.maximum(
                    new, score_part(key_ref, query_ref, bias_ref, scores_ref, n, part, own)
                )
            if n > 0:
                scores = scores_ref[n - 1, part * PART : (part + 1) * PART, :]
                totals[n - 1] += jnp.sum(jnp.exp2(scores - peaks[n - 1]), axis=0, keepdims=True)
        if n < blocks:
            totals[n] = totals[n] * jnp.exp2(old - new)
            peaks[n] = new
        if n > 0:
            finish(n - 1, peaks[n - 1], totals[n - 1])


def own_kernel(got_ref, turned_ref, peak_ref, total_ref, full_ref, bias_ref, scores_ref):
    full_rows(got_ref, full_ref)
    hide_keys(full_ref, bias_ref)

    def before(n):
        return jnp.full((1, BLOCK), PRIOR, jnp.float32), jnp.ones((1, BLOCK), jnp.float32)

    def finish(n, peak, total):
        peak_ref[:, n * BLOCK : (n + 1) * BLOCK] = peak
        total_ref[:, n * BLOCK : (n + 1) * BLOCK] = total

    fold(full_ref, full_ref, bias_ref, scores_ref, True, before, finish)
    turned_ref[...] = full_ref[...].T


def other_kernel(own_ref, got_ref, peak_ref, total_ref, density_ref, full_ref, bias_ref, scores_ref):
    full_rows(got_ref, full_ref)
    hide_keys(full_ref, bias_ref)

    def before(n):
        lanes = slice(n * BLOCK, (n + 1) * BLOCK)
        return peak_ref[:, lanes], total_ref[:, lanes]

    def finish(n, peak, total):
        density = peak * LN2 + jnp.log(total)
        for v in range(BLOCK // LANES):
            row = density[:, chunk_of(v)].reshape(1, 1, LANES)
            first = (n * BLOCK + v * LANES) // SLOTS
            density_ref[first : first + SHARED] = jnp.broadcast_to(row, (SHARED, 1, LANES))

    fold(full_ref, own_ref, bias_ref, scores_ref, False, before, finish)


def pick_kernel(returned_ref, slot_ref, density_ref):
    owners = returned_ref.shape[0]
    values = returned_ref[...].reshape(owners, LANES)
    slot = slot_ref[...]
    count = slot.shape[1]
    named = (iota((owners, count), 0) == slot // SLOTS).astype(jnp.bfloat16)
    turn = (SHARED - lax.axis_index("gx") % SHARED) % SHARED * SLOTS
    turned = pltpu.roll(values, turn, 1).T[:SLOTS]
    high = turned.astype(jnp.bfloat16)
    left = turned - high.astype(jnp.float32)
    middle = left.astype(jnp.bfloat16)
    low = (left - middle.astype(jnp.float32)).astype(jnp.bfloat16)
    picked = (dot(low, named) + dot(middle, named)) + dot(high, named)
    mine = iota((SLOTS, count), 0) == slot % SLOTS
    density_ref[...] = jnp.sum(jnp.where(mine, picked, 0.0), axis=0, keepdims=True)


def shards(embeddings, cluster):
    owners = lax.axis_size("gx")
    row_count, width = embeddings.shape
    main = width - LANES
    slot_count = owners * SLOTS
    send, slot = pl.pallas_call(
        pack_kernel,
        in_specs=[ANY_SPEC, ANY_SPEC],
        out_shape=(
            jax.ShapeDtypeStruct((slot_count, main), jnp.bfloat16),
            pltpu.VMEM((1, row_count), jnp.int32),
        ),
        scratch_shapes=[
            pltpu.VMEM((1, row_count), jnp.int32),
            pltpu.VMEM((row_count, width), jnp.bfloat16),
            pltpu.VMEM((slot_count, row_count), jnp.bfloat16),
            pltpu.SemaphoreType.DMA((COPIES + 1,)),
        ],
        compiler_params=PARAMS,
        name="pack",
    )(
        pltpu.with_memory_space_constraint(cluster.reshape(1, row_count), pltpu.HBM),
        pltpu.with_memory_space_constraint(embeddings, pltpu.HBM),
    )
    got = lax.all_to_all(
        send.reshape(owners, SLOTS, main), "gx", split_axis=0, concat_axis=0, tiled=True
    ).reshape(slot_count, main)
    other = lax.ppermute(got, "gy", [(0, 1), (1, 0)])
    own, peak, total = pl.pallas_call(
        own_kernel,
        in_specs=[VMEM_SPEC],
        out_shape=(
            pltpu.VMEM((width, slot_count), jnp.bfloat16),
            pltpu.VMEM((1, slot_count), jnp.float32),
            pltpu.VMEM((1, slot_count), jnp.float32),
        ),
        scratch_shapes=[
            pltpu.VMEM((slot_count, width), jnp.bfloat16),
            pltpu.VMEM((slot_count, LANES), jnp.float32),
            pltpu.VMEM((slot_count // BLOCK, slot_count, BLOCK), jnp.float32),
        ],
        compiler_params=PARAMS,
        name="own",
    )(on_chip(got))
    density = pl.pallas_call(
        other_kernel,
        in_specs=[VMEM_SPEC] * 4,
        out_shape=jax.ShapeDtypeStruct((owners, 1, LANES), jnp.float32),
        scratch_shapes=[
            pltpu.VMEM((slot_count, width), jnp.bfloat16),
            pltpu.VMEM((slot_count, LANES), jnp.float32),
            pltpu.VMEM((slot_count // BLOCK, slot_count, BLOCK), jnp.float32),
        ],
        compiler_params=PARAMS,
        name="other",
    )(on_chip(own), on_chip(other), on_chip(peak), on_chip(total))
    returned = lax.all_to_all(density, "gx", split_axis=0, concat_axis=0, tiled=True)
    picked = pl.pallas_call(
        pick_kernel,
        in_specs=[VMEM_SPEC, VMEM_SPEC],
        out_shape=jax.ShapeDtypeStruct((1, row_count), jnp.float32),
        compiler_params=PARAMS,
        name="pick",
    )(on_chip(returned), on_chip(slot))
    return picked.reshape(row_count)


def solution(mesh):
    return jax.shard_map(
        shards,
        mesh=mesh,
        in_specs=(P(("gx", "gy"), None), P(("gx", "gy"), None)),
        out_specs=P(("gx", "gy")),
        check_vma=False,
    )
```

```python
import math

import jax
import jax.numpy as jnp
from jax import lax
from jax.experimental import pallas as pl
from jax.experimental.pallas import tpu as pltpu
from jax.sharding import PartitionSpec as P

LOG2E = math.log2(math.e)
LN2 = math.log(2.0)
PRIOR = 6.0
ABSENT = 32.0
HIDDEN = -1e30
LANES = 128
SLOTS = 8
LAST = SLOTS - 1
SHARED = LANES // SLOTS
BLOCK = 512
PARTS = (512, 256)
COPIES = 1


def iota(shape, dim):
    return lax.broadcasted_iota(jnp.int32, shape, dim)


def dot(a, b):
    return jnp.dot(a, b, preferred_element_type=jnp.float32)


def dot_t(a, b):
    return lax.dot_general(a, b, (((1,), (1,)), ((), ())), preferred_element_type=jnp.float32)


def on_chip(x):
    return pltpu.with_memory_space_constraint(x, pltpu.VMEM)


def chunk_of(j):
    return slice(j * LANES, (j + 1) * LANES)


VMEM_SPEC = pl.BlockSpec(memory_space=pltpu.VMEM)
ANY_SPEC = pl.BlockSpec(memory_space=pl.ANY)
PARAMS = pltpu.CompilerParams(vmem_limit_bytes=16 << 20)


def pack_kernel(cluster_hbm, rows_hbm, send_ref, slot_ref, cluster_ref, rows_ref, place_ref, sems):
    row_count, width = rows_ref.shape
    part = row_count // COPIES
    ids_copy = pltpu.make_async_copy(cluster_hbm, cluster_ref, sems.at[COPIES])
    ids_copy.start()
    copies = []
    for n in range(COPIES):
        some = slice(n * part, (n + 1) * part)
        copies.append(pltpu.make_async_copy(rows_hbm.at[some, :], rows_ref.at[some, :], sems.at[n]))
        copies[n].start()
    count, main = send_ref.shape
    owners = count // SLOTS
    before = (iota((row_count, row_count), 0) < iota((row_count, row_count), 1)).astype(jnp.bfloat16)
    ids_copy.wait()
    ids = cluster_ref[...]
    named = iota((owners, row_count), 0) == ids
    earlier = dot(named.astype(jnp.bfloat16), before)
    rank = jnp.sum(jnp.where(named, earlier, 0.0), axis=0, keepdims=True).astype(jnp.int32)
    slot = ids * SLOTS + rank
    slot_ref[...] = slot
    some = 2 * SLOTS
    ahead = jnp.broadcast_to(slot, (some, row_count)) - iota((some, row_count), 0)
    ahead = ahead.astype(jnp.int16)
    for i in range(count // some):
        place_ref[i * some : (i + 1) * some, :] = jnp.where(
            ahead == i * some, jnp.ones((), jnp.bfloat16), jnp.zeros((), jnp.bfloat16)
        )
    members = jnp.sum(named.astype(jnp.float32), axis=1, keepdims=True)
    members = jnp.broadcast_to(members, (owners, LANES))[:, None, :]
    level = iota((owners, SLOTS, LANES), 1)
    rest = None
    for copy in copies:
        copy.wait()
    for n in reversed(range(width // (2 * LANES))):
        pair = dot(place_ref[...], rows_ref[:, 2 * n * LANES : 2 * (n + 1) * LANES])
        for j in (2 * n, 2 * n + 1):
            chunk = pair[:, (j % 2) * LANES : (j % 2 + 1) * LANES]
            if rest is None:
                rest = pair[:, LANES:].reshape(owners, SLOTS, LANES)
            if j * LANES == main:
                continue
            chunk = chunk.reshape(level.shape)
            if j == 0:
                empty = level.astype(jnp.float32) >= jnp.broadcast_to(members, level.shape)
                chunk = jnp.where(empty & (iota(level.shape, 2) == 0), ABSENT, chunk)
            chunk = jnp.where(level == LAST, pltpu.roll(rest, (LAST - j) % SLOTS, 1), chunk)
            send_ref[:, chunk_of(j)] = chunk.reshape(count, LANES).astype(jnp.bfloat16)


def full_rows(got_ref, full_ref):
    count, main = got_ref.shape
    shape = (count // SLOTS, SLOTS, LANES)
    level = iota(shape, 1)
    full_ref[:, :main] = got_ref[...]
    rest = jnp.zeros(shape, jnp.float32)
    for j in range(main // LANES):
        chunk = got_ref[:, chunk_of(j)].astype(jnp.float32).reshape(shape)
        rest = jnp.where(level == j, pltpu.roll(chunk, (j - LAST) % SLOTS, 1), rest)
    full_ref[:, main:] = rest.reshape(count, LANES).astype(jnp.bfloat16)


def hide_keys(full_ref, bias_ref):
    count = full_ref.shape[0]
    lead = full_ref[:, :LANES].astype(jnp.float32)[:, :1]
    level = iota((count, LANES), 0) % SLOTS
    bias_ref[...] = jnp.where((lead > 0.75 * ABSENT) | (level == LAST), HIDDEN, 0.0)


def score_part(key_ref, query_ref, bias_ref, scores_ref, n, keys, own):
    width = key_ref.shape[1]
    lanes = slice(n * BLOCK, (n + 1) * BLOCK)
    if own:
        scores = dot_t(key_ref[keys, :], query_ref[lanes, :])
    else:
        scores = dot(key_ref[keys, :], query_ref[:, lanes])
    bias = jnp.concatenate([bias_ref[keys, :]] * (BLOCK // LANES), axis=1)
    scores = scores * (LOG2E * width**-0.5) + bias
    if own and keys.start < lanes.stop and lanes.start < keys.stop:
        me = iota(scores.shape, 0) == iota(scores.shape, 1) + (lanes.start - keys.start)
        scores = jnp.where(me, HIDDEN, scores)
    scores_ref[n, keys, :] = scores
    return jnp.max(scores, axis=0, keepdims=True)


def fold(key_ref, query_ref, bias_ref, scores_ref, own, before, finish):
    count = key_ref.shape[0]
    blocks, size = count // BLOCK, PARTS[0 if own else 1]
    parts = [slice(k, k + size) for k in range(0, count, size)]
    peaks, totals = {}, {}
    for n in range(blocks + 1):
        if n < blocks:
            peaks[n], totals[n] = before(n)
            old, new = peaks[n], peaks[n]
        for keys in parts:
            if n < blocks:
                new = jnp.maximum(
                    new, score_part(key_ref, query_ref, bias_ref, scores_ref, n, keys, own)
                )
            if n > 0:
                scores = scores_ref[n - 1, keys, :]
                totals[n - 1] += jnp.sum(jnp.exp2(scores - peaks[n - 1]), axis=0, keepdims=True)
        if n < blocks:
            totals[n] = totals[n] * jnp.exp2(old - new)
            peaks[n] = new
        if n > 0:
            finish(n - 1, peaks[n - 1], totals[n - 1])


def own_kernel(got_ref, turned_ref, peak_ref, total_ref, full_ref, bias_ref, scores_ref):
    full_rows(got_ref, full_ref)
    hide_keys(full_ref, bias_ref)

    def before(n):
        return jnp.full((1, BLOCK), PRIOR, jnp.float32), jnp.ones((1, BLOCK), jnp.float32)

    def finish(n, peak, total):
        peak_ref[:, n * BLOCK : (n + 1) * BLOCK] = peak
        total_ref[:, n * BLOCK : (n + 1) * BLOCK] = total

    fold(full_ref, full_ref, bias_ref, scores_ref, True, before, finish)
    turned_ref[...] = full_ref[...].T


def other_kernel(own_ref, got_ref, peak_ref, total_ref, density_ref, full_ref, bias_ref, scores_ref):
    full_rows(got_ref, full_ref)
    hide_keys(full_ref, bias_ref)

    def before(n):
        lanes = slice(n * BLOCK, (n + 1) * BLOCK)
        return peak_ref[:, lanes], total_ref[:, lanes]

    def finish(n, peak, total):
        density = peak * LN2 + jnp.log(total)
        for v in range(BLOCK // LANES):
            row = density[:, chunk_of(v)].reshape(1, 1, LANES)
            first = (n * BLOCK + v * LANES) // SLOTS
            density_ref[first : first + SHARED] = jnp.broadcast_to(row, (SHARED, 1, LANES))

    fold(full_ref, own_ref, bias_ref, scores_ref, False, before, finish)


def pick_kernel(returned_ref, slot_ref, density_ref):
    owners = returned_ref.shape[0]
    values = returned_ref[...].reshape(owners, LANES)
    slot = slot_ref[...]
    count = slot.shape[1]
    named = (iota((owners, count), 0) == slot // SLOTS).astype(jnp.bfloat16)
    turn = (SHARED - lax.axis_index("gx") % SHARED) % SHARED * SLOTS
    turned = pltpu.roll(values, turn, 1).T[:SLOTS]
    high = turned.astype(jnp.bfloat16)
    left = turned - high.astype(jnp.float32)
    middle = left.astype(jnp.bfloat16)
    low = (left - middle.astype(jnp.float32)).astype(jnp.bfloat16)
    picked = (dot(low, named) + dot(middle, named)) + dot(high, named)
    mine = iota((SLOTS, count), 0) == slot % SLOTS
    density_ref[...] = jnp.sum(jnp.where(mine, picked, 0.0), axis=0, keepdims=True)


def shards(embeddings, cluster):
    owners = lax.axis_size("gx")
    row_count, width = embeddings.shape
    main = width - LANES
    slot_count = owners * SLOTS
    send, slot = pl.pallas_call(
        pack_kernel,
        in_specs=[ANY_SPEC, ANY_SPEC],
        out_shape=(
            jax.ShapeDtypeStruct((slot_count, main), jnp.bfloat16),
            pltpu.VMEM((1, row_count), jnp.int32),
        ),
        scratch_shapes=[
            pltpu.VMEM((1, row_count), jnp.int32),
            pltpu.VMEM((row_count, width), jnp.bfloat16),
            pltpu.VMEM((slot_count, row_count), jnp.bfloat16),
            pltpu.SemaphoreType.DMA((COPIES + 1,)),
        ],
        compiler_params=PARAMS,
        name="pack",
    )(
        pltpu.with_memory_space_constraint(cluster.reshape(1, row_count), pltpu.HBM),
        pltpu.with_memory_space_constraint(embeddings, pltpu.HBM),
    )
    got = lax.all_to_all(
        send.reshape(owners, SLOTS, main), "gx", split_axis=0, concat_axis=0, tiled=True
    ).reshape(slot_count, main)
    other = lax.ppermute(got, "gy", [(0, 1), (1, 0)])
    own, peak, total = pl.pallas_call(
        own_kernel,
        in_specs=[VMEM_SPEC],
        out_shape=(
            pltpu.VMEM((width, slot_count), jnp.bfloat16),
            pltpu.VMEM((1, slot_count), jnp.float32),
            pltpu.VMEM((1, slot_count), jnp.float32),
        ),
        scratch_shapes=[
            pltpu.VMEM((slot_count, width), jnp.bfloat16),
            pltpu.VMEM((slot_count, LANES), jnp.float32),
            pltpu.VMEM((slot_count // BLOCK, slot_count, BLOCK), jnp.float32),
        ],
        compiler_params=PARAMS,
        name="own",
    )(on_chip(got))
    density = pl.pallas_call(
        other_kernel,
        in_specs=[VMEM_SPEC] * 4,
        out_shape=jax.ShapeDtypeStruct((owners, 1, LANES), jnp.float32),
        scratch_shapes=[
            pltpu.VMEM((slot_count, width), jnp.bfloat16),
            pltpu.VMEM((slot_count, LANES), jnp.float32),
            pltpu.VMEM((slot_count // BLOCK, slot_count, BLOCK), jnp.float32),
        ],
        compiler_params=PARAMS,
        name="other",
    )(on_chip(own), on_chip(other), on_chip(peak), on_chip(total))
    returned = lax.all_to_all(density, "gx", split_axis=0, concat_axis=0, tiled=True)
    picked = pl.pallas_call(
        pick_kernel,
        in_specs=[VMEM_SPEC, VMEM_SPEC],
        out_shape=jax.ShapeDtypeStruct((1, row_count), jnp.float32),
        compiler_params=PARAMS,
        name="pick",
    )(on_chip(returned), on_chip(slot))
    return picked.reshape(row_count)


def solution(mesh):
    return jax.shard_map(
        shards,
        mesh=mesh,
        in_specs=(P(("gx", "gy"), None), P(("gx", "gy"), None)),
        out_specs=P(("gx", "gy")),
        check_vma=False,
    )
```

```python
import math

import jax
import jax.numpy as jnp
from jax import lax
from jax.experimental import pallas as pl
from jax.experimental.pallas import tpu as pltpu
from jax.sharding import PartitionSpec as P

LOG2E = math.log2(math.e)
LN2 = math.log(2.0)
PRIOR = 6.0
ABSENT = 32.0
HIDDEN = -1e30
LANES = 128
SLOTS = 8
LAST = SLOTS - 1
SHARED = LANES // SLOTS
BLOCK = 512
PARTS = (512, 256)
COPIES = 1


def iota(shape, dim):
    return lax.broadcasted_iota(jnp.int32, shape, dim)


def dot(a, b):
    return jnp.dot(a, b, preferred_element_type=jnp.float32)


def dot_t(a, b):
    return lax.dot_general(a, b, (((1,), (1,)), ((), ())), preferred_element_type=jnp.float32)


def on_chip(x):
    return pltpu.with_memory_space_constraint(x, pltpu.VMEM)


def chunk_of(j):
    return slice(j * LANES, (j + 1) * LANES)


VMEM_SPEC = pl.BlockSpec(memory_space=pltpu.VMEM)
ANY_SPEC = pl.BlockSpec(memory_space=pl.ANY)
PARAMS = pltpu.CompilerParams(vmem_limit_bytes=16 << 20)


def pack_kernel(cluster_hbm, rows_hbm, send_ref, slot_ref, cluster_ref, rows_ref, place_ref, sems):
    row_count, width = rows_ref.shape
    part = row_count // COPIES
    ids_copy = pltpu.make_async_copy(cluster_hbm, cluster_ref, sems.at[COPIES])
    ids_copy.start()
    copies = []
    for n in range(COPIES):
        some = slice(n * part, (n + 1) * part)
        copies.append(pltpu.make_async_copy(rows_hbm.at[some, :], rows_ref.at[some, :], sems.at[n]))
        copies[n].start()
    count, main = send_ref.shape
    owners = count // SLOTS
    before = (iota((row_count, row_count), 0) < iota((row_count, row_count), 1)).astype(jnp.bfloat16)
    ids_copy.wait()
    ids = cluster_ref[...]
    named = iota((owners, row_count), 0) == ids
    earlier = dot(named.astype(jnp.bfloat16), before)
    rank = jnp.sum(jnp.where(named, earlier, 0.0), axis=0, keepdims=True).astype(jnp.int32)
    slot = ids * SLOTS + rank
    slot_ref[...] = slot
    some = 2 * SLOTS
    ahead = jnp.broadcast_to(slot, (some, row_count)) - iota((some, row_count), 0)
    ahead = ahead.astype(jnp.int16)
    for i in range(count // some):
        place_ref[i * some : (i + 1) * some, :] = jnp.where(
            ahead == i * some, jnp.ones((), jnp.bfloat16), jnp.zeros((), jnp.bfloat16)
        )
    members = jnp.sum(named.astype(jnp.float32), axis=1, keepdims=True)
    members = jnp.broadcast_to(members, (owners, LANES))[:, None, :]
    level = iota((owners, SLOTS, LANES), 1)
    rest = None
    for copy in copies:
        copy.wait()
    for n in reversed(range(width // (2 * LANES))):
        pair = dot(place_ref[...], rows_ref[:, 2 * n * LANES : 2 * (n + 1) * LANES])
        for j in (2 * n, 2 * n + 1):
            chunk = pair[:, (j % 2) * LANES : (j % 2 + 1) * LANES]
            if rest is None:
                rest = pair[:, LANES:].reshape(owners, SLOTS, LANES)
            if j * LANES == main:
                continue
            chunk = chunk.reshape(level.shape)
            if j == 0:
                empty = level.astype(jnp.float32) >= jnp.broadcast_to(members, level.shape)
                chunk = jnp.where(empty & (iota(level.shape, 2) == 0), ABSENT, chunk)
            chunk = jnp.where(level == LAST, pltpu.roll(rest, (LAST - j) % SLOTS, 1), chunk)
            send_ref[:, chunk_of(j)] = chunk.reshape(count, LANES).astype(jnp.bfloat16)


def full_rows(got_ref, full_ref):
    count, main = got_ref.shape
    shape = (count // SLOTS, SLOTS, LANES)
    level = iota(shape, 1)
    full_ref[:, :main] = got_ref[...]
    rest = jnp.zeros(shape, jnp.float32)
    for j in range(main // LANES):
        chunk = got_ref[:, chunk_of(j)].astype(jnp.float32).reshape(shape)
        rest = jnp.where(level == j, jnp.broadcast_to(chunk[:, LAST:, :], shape), rest)
    full_ref[:, main:] = rest.reshape(count, LANES).astype(jnp.bfloat16)


def hide_keys(full_ref, bias_ref):
    count = full_ref.shape[0]
    lead = full_ref[:, :LANES].astype(jnp.float32)[:, :1]
    level = iota((count, LANES), 0) % SLOTS
    bias_ref[...] = jnp.where((lead > 0.75 * ABSENT) | (level == LAST), HIDDEN, 0.0)


def score_part(key_ref, query_ref, bias_ref, scores_ref, n, keys, own):
    width = key_ref.shape[1]
    lanes = slice(n * BLOCK, (n + 1) * BLOCK)
    if own:
        scores = dot_t(key_ref[keys, :], query_ref[lanes, :])
    else:
        scores = dot(key_ref[keys, :], query_ref[:, lanes])
    bias = jnp.concatenate([bias_ref[keys, :]] * (BLOCK // LANES), axis=1)
    scores = scores * (LOG2E * width**-0.5) + bias
    if own and keys.start < lanes.stop and lanes.start < keys.stop:
        me = iota(scores.shape, 0) == iota(scores.shape, 1) + (lanes.start - keys.start)
        scores = jnp.where(me, HIDDEN, scores)
    scores_ref[n, keys, :] = scores
    return jnp.max(scores, axis=0, keepdims=True)


def fold(key_ref, query_ref, bias_ref, scores_ref, own, before, finish):
    count = key_ref.shape[0]
    blocks, size = count // BLOCK, PARTS[0 if own else 1]
    parts = [slice(k, k + size) for k in range(0, count, size)]
    peaks, totals = {}, {}
    for n in range(blocks + 1):
        if n < blocks:
            peaks[n], totals[n] = before(n)
            old, new = peaks[n], peaks[n]
        for keys in parts:
            if n < blocks:
                new = jnp.maximum(
                    new, score_part(key_ref, query_ref, bias_ref, scores_ref, n, keys, own)
                )
            if n > 0:
                scores = scores_ref[n - 1, keys, :]
                totals[n - 1] += jnp.sum(jnp.exp2(scores - peaks[n - 1]), axis=0, keepdims=True)
        if n < blocks:
            totals[n] = totals[n] * jnp.exp2(old - new)
            peaks[n] = new
        if n > 0:
            finish(n - 1, peaks[n - 1], totals[n - 1])


def own_kernel(got_ref, turned_ref, peak_ref, total_ref, full_ref, bias_ref, scores_ref):
    full_rows(got_ref, full_ref)
    hide_keys(full_ref, bias_ref)

    def before(n):
        return jnp.full((1, BLOCK), PRIOR, jnp.float32), jnp.ones((1, BLOCK), jnp.float32)

    def finish(n, peak, total):
        peak_ref[:, n * BLOCK : (n + 1) * BLOCK] = peak
        total_ref[:, n * BLOCK : (n + 1) * BLOCK] = total

    fold(full_ref, full_ref, bias_ref, scores_ref, True, before, finish)
    turned_ref[...] = full_ref[...].T


def other_kernel(own_ref, got_ref, peak_ref, total_ref, density_ref, full_ref, bias_ref, scores_ref):
    full_rows(got_ref, full_ref)
    hide_keys(full_ref, bias_ref)

    def before(n):
        lanes = slice(n * BLOCK, (n + 1) * BLOCK)
        return peak_ref[:, lanes], total_ref[:, lanes]

    def finish(n, peak, total):
        density = peak * LN2 + jnp.log(total)
        for v in range(BLOCK // LANES):
            row = density[:, chunk_of(v)].reshape(1, 1, LANES)
            first = (n * BLOCK + v * LANES) // SLOTS
            density_ref[first : first + SHARED] = jnp.broadcast_to(row, (SHARED, 1, LANES))

    fold(full_ref, own_ref, bias_ref, scores_ref, False, before, finish)


def pick_kernel(returned_ref, slot_ref, density_ref):
    owners = returned_ref.shape[0]
    values = returned_ref[...].reshape(owners, LANES)
    slot = slot_ref[...]
    count = slot.shape[1]
    named = (iota((owners, count), 0) == slot // SLOTS).astype(jnp.bfloat16)
    turn = (SHARED - lax.axis_index("gx") % SHARED) % SHARED * SLOTS
    turned = pltpu.roll(values, turn, 1).T[:SLOTS]
    high = turned.astype(jnp.bfloat16)
    left = turned - high.astype(jnp.float32)
    middle = left.astype(jnp.bfloat16)
    low = (left - middle.astype(jnp.float32)).astype(jnp.bfloat16)
    picked = (dot(low, named) + dot(middle, named)) + dot(high, named)
    mine = iota((SLOTS, count), 0) == slot % SLOTS
    density_ref[...] = jnp.sum(jnp.where(mine, picked, 0.0), axis=0, keepdims=True)


def shards(embeddings, cluster):
    owners = lax.axis_size("gx")
    row_count, width = embeddings.shape
    main = width - LANES
    slot_count = owners * SLOTS
    send, slot = pl.pallas_call(
        pack_kernel,
        in_specs=[ANY_SPEC, ANY_SPEC],
        out_shape=(
            jax.ShapeDtypeStruct((slot_count, main), jnp.bfloat16),
            pltpu.VMEM((1, row_count), jnp.int32),
        ),
        scratch_shapes=[
            pltpu.VMEM((1, row_count), jnp.int32),
            pltpu.VMEM((row_count, width), jnp.bfloat16),
            pltpu.VMEM((slot_count, row_count), jnp.bfloat16),
            pltpu.SemaphoreType.DMA((COPIES + 1,)),
        ],
        compiler_params=PARAMS,
        name="pack",
    )(
        pltpu.with_memory_space_constraint(cluster.reshape(1, row_count), pltpu.HBM),
        pltpu.with_memory_space_constraint(embeddings, pltpu.HBM),
    )
    got = lax.all_to_all(
        send.reshape(owners, SLOTS, main), "gx", split_axis=0, concat_axis=0, tiled=True
    ).reshape(slot_count, main)
    other = lax.ppermute(got, "gy", [(0, 1), (1, 0)])
    own, peak, total = pl.pallas_call(
        own_kernel,
        in_specs=[VMEM_SPEC],
        out_shape=(
            pltpu.VMEM((width, slot_count), jnp.bfloat16),
            pltpu.VMEM((1, slot_count), jnp.float32),
            pltpu.VMEM((1, slot_count), jnp.float32),
        ),
        scratch_shapes=[
            pltpu.VMEM((slot_count, width), jnp.bfloat16),
            pltpu.VMEM((slot_count, LANES), jnp.float32),
            pltpu.VMEM((slot_count // BLOCK, slot_count, BLOCK), jnp.float32),
        ],
        compiler_params=PARAMS,
        name="own",
    )(on_chip(got))
    density = pl.pallas_call(
        other_kernel,
        in_specs=[VMEM_SPEC] * 4,
        out_shape=jax.ShapeDtypeStruct((owners, 1, LANES), jnp.float32),
        scratch_shapes=[
            pltpu.VMEM((slot_count, width), jnp.bfloat16),
            pltpu.VMEM((slot_count, LANES), jnp.float32),
            pltpu.VMEM((slot_count // BLOCK, slot_count, BLOCK), jnp.float32),
        ],
        compiler_params=PARAMS,
        name="other",
    )(on_chip(own), on_chip(other), on_chip(peak), on_chip(total))
    returned = lax.all_to_all(density, "gx", split_axis=0, concat_axis=0, tiled=True)
    picked = pl.pallas_call(
        pick_kernel,
        in_specs=[VMEM_SPEC, VMEM_SPEC],
        out_shape=jax.ShapeDtypeStruct((1, row_count), jnp.float32),
        compiler_params=PARAMS,
        name="pick",
    )(on_chip(returned), on_chip(slot))
    return picked.reshape(row_count)


def solution(mesh):
    return jax.shard_map(
        shards,
        mesh=mesh,
        in_specs=(P(("gx", "gy"), None), P(("gx", "gy"), None)),
        out_specs=P(("gx", "gy")),
        check_vma=False,
    )
```

```python
import math

import jax
import jax.numpy as jnp
from jax import lax
from jax.experimental import pallas as pl
from jax.experimental.pallas import tpu as pltpu
from jax.sharding import PartitionSpec as P

LOG2E = math.log2(math.e)
LN2 = math.log(2.0)
PRIOR = 6.0
ABSENT = 32.0
HIDDEN = -1e30
LANES = 128
SLOTS = 8
LAST = SLOTS - 1
SHARED = LANES // SLOTS
BLOCK = 512
PARTS = (512, 256)
COPIES = 1


def iota(shape, dim):
    return lax.broadcasted_iota(jnp.int32, shape, dim)


def dot(a, b):
    return jnp.dot(a, b, preferred_element_type=jnp.float32)


def dot_t(a, b):
    return lax.dot_general(a, b, (((1,), (1,)), ((), ())), preferred_element_type=jnp.float32)


def on_chip(x):
    return pltpu.with_memory_space_constraint(x, pltpu.VMEM)


def chunk_of(j):
    return slice(j * LANES, (j + 1) * LANES)


VMEM_SPEC = pl.BlockSpec(memory_space=pltpu.VMEM)
ANY_SPEC = pl.BlockSpec(memory_space=pl.ANY)
PARAMS = pltpu.CompilerParams(vmem_limit_bytes=16 << 20)


def pack_kernel(cluster_hbm, rows_hbm, send_ref, slot_ref, cluster_ref, rows_ref, place_ref, sems):
    row_count, width = rows_ref.shape
    part = row_count // COPIES
    ids_copy = pltpu.make_async_copy(cluster_hbm, cluster_ref, sems.at[COPIES])
    ids_copy.start()
    copies = []
    for n in range(COPIES):
        some = slice(n * part, (n + 1) * part)
        copies.append(pltpu.make_async_copy(rows_hbm.at[some, :], rows_ref.at[some, :], sems.at[n]))
        copies[n].start()
    count, main = send_ref.shape
    owners = count // SLOTS
    before = (iota((row_count, row_count), 0) < iota((row_count, row_count), 1)).astype(jnp.bfloat16)
    ids_copy.wait()
    ids = cluster_ref[...]
    named = iota((owners, row_count), 0) == ids
    earlier = dot(named.astype(jnp.bfloat16), before)
    rank = jnp.sum(jnp.where(named, earlier, 0.0), axis=0, keepdims=True).astype(jnp.int32)
    slot = ids * SLOTS + rank
    slot_ref[...] = slot
    some = 2 * SLOTS
    ahead = jnp.broadcast_to(slot, (some, row_count)) - iota((some, row_count), 0)
    ahead = ahead.astype(jnp.int16)
    for i in range(count // some):
        place_ref[i * some : (i + 1) * some, :] = jnp.where(
            ahead == i * some, jnp.ones((), jnp.bfloat16), jnp.zeros((), jnp.bfloat16)
        )
    members = jnp.sum(named.astype(jnp.float32), axis=1, keepdims=True)
    members = jnp.broadcast_to(members, (owners, LANES))[:, None, :]
    level = iota((owners, SLOTS, LANES), 1)
    rest = None
    for copy in copies:
        copy.wait()
    for n in reversed(range(width // (2 * LANES))):
        pair = dot(place_ref[...], rows_ref[:, 2 * n * LANES : 2 * (n + 1) * LANES])
        for j in (2 * n, 2 * n + 1):
            chunk = pair[:, (j % 2) * LANES : (j % 2 + 1) * LANES]
            if rest is None:
                rest = pair[:, LANES:].reshape(owners, SLOTS, LANES)
            if j * LANES == main:
                continue
            chunk = chunk.reshape(level.shape)
            if j == 0:
                empty = level.astype(jnp.float32) >= jnp.broadcast_to(members, level.shape)
                chunk = jnp.where(empty & (iota(level.shape, 2) == 0), ABSENT, chunk)
            chunk = jnp.where(level == LAST, jnp.broadcast_to(rest[:, j : j + 1, :], level.shape), chunk)
            send_ref[:, chunk_of(j)] = chunk.reshape(count, LANES).astype(jnp.bfloat16)


def full_rows(got_ref, full_ref):
    count, main = got_ref.shape
    shape = (count // SLOTS, SLOTS, LANES)
    level = iota(shape, 1)
    full_ref[:, :main] = got_ref[...]
    rest = jnp.zeros(shape, jnp.float32)
    for j in range(main // LANES):
        chunk = got_ref[:, chunk_of(j)].astype(jnp.float32).reshape(shape)
        rest = jnp.where(level == j, jnp.broadcast_to(chunk[:, LAST:, :], shape), rest)
    full_ref[:, main:] = rest.reshape(count, LANES).astype(jnp.bfloat16)


def hide_keys(full_ref, bias_ref):
    count = full_ref.shape[0]
    lead = full_ref[:, :LANES].astype(jnp.float32)[:, :1]
    level = iota((count, LANES), 0) % SLOTS
    bias_ref[...] = jnp.where((lead > 0.75 * ABSENT) | (level == LAST), HIDDEN, 0.0)


def score_part(key_ref, query_ref, bias_ref, scores_ref, n, keys, own):
    width = key_ref.shape[1]
    lanes = slice(n * BLOCK, (n + 1) * BLOCK)
    if own:
        scores = dot_t(key_ref[keys, :], query_ref[lanes, :])
    else:
        scores = dot(key_ref[keys, :], query_ref[:, lanes])
    bias = jnp.concatenate([bias_ref[keys, :]] * (BLOCK // LANES), axis=1)
    scores = scores * (LOG2E * width**-0.5) + bias
    if own and keys.start < lanes.stop and lanes.start < keys.stop:
        me = iota(scores.shape, 0) == iota(scores.shape, 1) + (lanes.start - keys.start)
        scores = jnp.where(me, HIDDEN, scores)
    scores_ref[n, keys, :] = scores
    return jnp.max(scores, axis=0, keepdims=True)


def fold(key_ref, query_ref, bias_ref, scores_ref, own, before, finish):
    count = key_ref.shape[0]
    blocks, size = count // BLOCK, PARTS[0 if own else 1]
    parts = [slice(k, k + size) for k in range(0, count, size)]
    peaks, totals = {}, {}
    for n in range(blocks + 1):
        if n < blocks:
            peaks[n], totals[n] = before(n)
            old, new = peaks[n], peaks[n]
        for keys in parts:
            if n < blocks:
                new = jnp.maximum(
                    new, score_part(key_ref, query_ref, bias_ref, scores_ref, n, keys, own)
                )
            if n > 0:
                scores = scores_ref[n - 1, keys, :]
                totals[n - 1] += jnp.sum(jnp.exp2(scores - peaks[n - 1]), axis=0, keepdims=True)
        if n < blocks:
            totals[n] = totals[n] * jnp.exp2(old - new)
            peaks[n] = new
        if n > 0:
            finish(n - 1, peaks[n - 1], totals[n - 1])


def own_kernel(got_ref, turned_ref, peak_ref, total_ref, full_ref, bias_ref, scores_ref):
    full_rows(got_ref, full_ref)
    hide_keys(full_ref, bias_ref)

    def before(n):
        return jnp.full((1, BLOCK), PRIOR, jnp.float32), jnp.ones((1, BLOCK), jnp.float32)

    def finish(n, peak, total):
        peak_ref[:, n * BLOCK : (n + 1) * BLOCK] = peak
        total_ref[:, n * BLOCK : (n + 1) * BLOCK] = total

    fold(full_ref, full_ref, bias_ref, scores_ref, True, before, finish)
    turned_ref[...] = full_ref[...].T


def other_kernel(own_ref, got_ref, peak_ref, total_ref, density_ref, full_ref, bias_ref, scores_ref):
    full_rows(got_ref, full_ref)
    hide_keys(full_ref, bias_ref)

    def before(n):
        lanes = slice(n * BLOCK, (n + 1) * BLOCK)
        return peak_ref[:, lanes], total_ref[:, lanes]

    def finish(n, peak, total):
        density = peak * LN2 + jnp.log(total)
        for v in range(BLOCK // LANES):
            row = density[:, chunk_of(v)].reshape(1, 1, LANES)
            first = (n * BLOCK + v * LANES) // SLOTS
            density_ref[first : first + SHARED] = jnp.broadcast_to(row, (SHARED, 1, LANES))

    fold(full_ref, own_ref, bias_ref, scores_ref, False, before, finish)


def pick_kernel(returned_ref, slot_ref, density_ref):
    owners = returned_ref.shape[0]
    values = returned_ref[...].reshape(owners, LANES)
    slot = slot_ref[...]
    count = slot.shape[1]
    named = (iota((owners, count), 0) == slot // SLOTS).astype(jnp.bfloat16)
    turn = (SHARED - lax.axis_index("gx") % SHARED) % SHARED * SLOTS
    turned = pltpu.roll(values, turn, 1).T[:SLOTS]
    high = turned.astype(jnp.bfloat16)
    left = turned - high.astype(jnp.float32)
    middle = left.astype(jnp.bfloat16)
    low = (left - middle.astype(jnp.float32)).astype(jnp.bfloat16)
    picked = (dot(low, named) + dot(middle, named)) + dot(high, named)
    mine = iota((SLOTS, count), 0) == slot % SLOTS
    density_ref[...] = jnp.sum(jnp.where(mine, picked, 0.0), axis=0, keepdims=True)


def shards(embeddings, cluster):
    owners = lax.axis_size("gx")
    row_count, width = embeddings.shape
    main = width - LANES
    slot_count = owners * SLOTS
    send, slot = pl.pallas_call(
        pack_kernel,
        in_specs=[ANY_SPEC, ANY_SPEC],
        out_shape=(
            jax.ShapeDtypeStruct((slot_count, main), jnp.bfloat16),
            pltpu.VMEM((1, row_count), jnp.int32),
        ),
        scratch_shapes=[
            pltpu.VMEM((1, row_count), jnp.int32),
            pltpu.VMEM((row_count, width), jnp.bfloat16),
            pltpu.VMEM((slot_count, row_count), jnp.bfloat16),
            pltpu.SemaphoreType.DMA((COPIES + 1,)),
        ],
        compiler_params=PARAMS,
        name="pack",
    )(
        pltpu.with_memory_space_constraint(cluster.reshape(1, row_count), pltpu.HBM),
        pltpu.with_memory_space_constraint(embeddings, pltpu.HBM),
    )
    got = lax.all_to_all(
        send.reshape(owners, SLOTS, main), "gx", split_axis=0, concat_axis=0, tiled=True
    ).reshape(slot_count, main)
    other = lax.ppermute(got, "gy", [(0, 1), (1, 0)])
    own, peak, total = pl.pallas_call(
        own_kernel,
        in_specs=[VMEM_SPEC],
        out_shape=(
            pltpu.VMEM((width, slot_count), jnp.bfloat16),
            pltpu.VMEM((1, slot_count), jnp.float32),
            pltpu.VMEM((1, slot_count), jnp.float32),
        ),
        scratch_shapes=[
            pltpu.VMEM((slot_count, width), jnp.bfloat16),
            pltpu.VMEM((slot_count, LANES), jnp.float32),
            pltpu.VMEM((slot_count // BLOCK, slot_count, BLOCK), jnp.float32),
        ],
        compiler_params=PARAMS,
        name="own",
    )(on_chip(got))
    density = pl.pallas_call(
        other_kernel,
        in_specs=[VMEM_SPEC] * 4,
        out_shape=jax.ShapeDtypeStruct((owners, 1, LANES), jnp.float32),
        scratch_shapes=[
            pltpu.VMEM((slot_count, width), jnp.bfloat16),
            pltpu.VMEM((slot_count, LANES), jnp.float32),
            pltpu.VMEM((slot_count // BLOCK, slot_count, BLOCK), jnp.float32),
        ],
        compiler_params=PARAMS,
        name="other",
    )(on_chip(own), on_chip(other), on_chip(peak), on_chip(total))
    returned = lax.all_to_all(density, "gx", split_axis=0, concat_axis=0, tiled=True)
    picked = pl.pallas_call(
        pick_kernel,
        in_specs=[VMEM_SPEC, VMEM_SPEC],
        out_shape=jax.ShapeDtypeStruct((1, row_count), jnp.float32),
        compiler_params=PARAMS,
        name="pick",
    )(on_chip(returned), on_chip(slot))
    return picked.reshape(row_count)


def solution(mesh):
    return jax.shard_map(
        shards,
        mesh=mesh,
        in_specs=(P(("gx", "gy"), None), P(("gx", "gy"), None)),
        out_specs=P(("gx", "gy")),
        check_vma=False,
    )
```

```python
import math

import jax
import jax.numpy as jnp
from jax import lax
from jax.experimental import pallas as pl
from jax.experimental.pallas import tpu as pltpu
from jax.sharding import PartitionSpec as P

LOG2E = math.log2(math.e)
LN2 = math.log(2.0)
PRIOR = 6.0
ABSENT = 32.0
HIDDEN = -1e30
LANES = 128
SLOTS = 8
LAST = SLOTS - 1
SHARED = LANES // SLOTS
BLOCK = 512
PARTS = (512, 256)
COPIES = 1


def iota(shape, dim):
    return lax.broadcasted_iota(jnp.int32, shape, dim)


def dot(a, b):
    return jnp.dot(a, b, preferred_element_type=jnp.float32)


def dot_t(a, b):
    return lax.dot_general(a, b, (((1,), (1,)), ((), ())), preferred_element_type=jnp.float32)


def on_chip(x):
    return pltpu.with_memory_space_constraint(x, pltpu.VMEM)


def chunk_of(j):
    return slice(j * LANES, (j + 1) * LANES)


VMEM_SPEC = pl.BlockSpec(memory_space=pltpu.VMEM)
ANY_SPEC = pl.BlockSpec(memory_space=pl.ANY)
PARAMS = pltpu.CompilerParams(vmem_limit_bytes=16 << 20)


def pack_kernel(cluster_hbm, rows_hbm, send_ref, slot_ref, cluster_ref, rows_ref, place_ref, sems):
    row_count, width = rows_ref.shape
    part = row_count // COPIES
    ids_copy = pltpu.make_async_copy(cluster_hbm, cluster_ref, sems.at[COPIES])
    ids_copy.start()
    copies = []
    for n in range(COPIES):
        some = slice(n * part, (n + 1) * part)
        copies.append(pltpu.make_async_copy(rows_hbm.at[some, :], rows_ref.at[some, :], sems.at[n]))
        copies[n].start()
    count, main = send_ref.shape
    owners = count // SLOTS
    before = (iota((row_count, row_count), 0) < iota((row_count, row_count), 1)).astype(jnp.bfloat16)
    ids_copy.wait()
    ids = cluster_ref[...]
    named = iota((owners, row_count), 0) == ids
    earlier = dot(named.astype(jnp.bfloat16), before)
    rank = jnp.sum(jnp.where(named, earlier, 0.0), axis=0, keepdims=True).astype(jnp.int32)
    slot = ids * SLOTS + rank
    slot_ref[...] = slot
    some = 2 * SLOTS
    ahead = jnp.broadcast_to(slot, (some, row_count)) - iota((some, row_count), 0)
    ahead = ahead.astype(jnp.int16)
    for i in range(count // some):
        place_ref[i * some : (i + 1) * some, :] = jnp.where(
            ahead == i * some, jnp.ones((), jnp.bfloat16), jnp.zeros((), jnp.bfloat16)
        )
    members = jnp.sum(named.astype(jnp.float32), axis=1, keepdims=True)
    members = jnp.broadcast_to(members, (owners, LANES))[:, None, :]
    level = iota((owners, SLOTS, LANES), 1)
    rest = None
    for copy in copies:
        copy.wait()
    for n in reversed(range(width // (2 * LANES))):
        pair = dot(place_ref[...], rows_ref[:, 2 * n * LANES : 2 * (n + 1) * LANES])
        for j in (2 * n, 2 * n + 1):
            chunk = pair[:, (j % 2) * LANES : (j % 2 + 1) * LANES]
            if rest is None:
                rest = pair[:, LANES:].reshape(owners, SLOTS, LANES)
            if j * LANES == main:
                continue
            chunk = chunk.reshape(level.shape)
            if j == 0:
                empty = level.astype(jnp.float32) >= jnp.broadcast_to(members, level.shape)
                chunk = jnp.where(empty & (iota(level.shape, 2) == 0), ABSENT, chunk)
            chunk = jnp.where(level == LAST, pltpu.roll(rest, (LAST - j) % SLOTS, 1), chunk)
            send_ref[:, chunk_of(j)] = chunk.reshape(count, LANES).astype(jnp.bfloat16)


def full_rows(got_ref, full_ref):
    count, main = got_ref.shape
    shape = (count // SLOTS, SLOTS, LANES)
    level = iota(shape, 1)
    full_ref[:, :main] = got_ref[...]
    rest = jnp.zeros(shape, jnp.float32)
    for j in range(main // LANES):
        chunk = got_ref[:, chunk_of(j)].astype(jnp.float32).reshape(shape)
        rest = jnp.where(level == j, jnp.broadcast_to(chunk[:, LAST:, :], shape), rest)
    full_ref[:, main:] = rest.reshape(count, LANES).astype(jnp.bfloat16)


def hide_keys(full_ref, bias_ref):
    count = full_ref.shape[0]
    lead = full_ref[:, :LANES].astype(jnp.float32)[:, :1]
    level = iota((count, LANES), 0) % SLOTS
    bias_ref[...] = jnp.where((lead > 0.75 * ABSENT) | (level == LAST), HIDDEN, 0.0)


def score_part(key_ref, query_ref, bias_ref, scores_ref, n, keys, own):
    width = key_ref.shape[1]
    lanes = slice(n * BLOCK, (n + 1) * BLOCK)
    if own:
        scores = dot_t(key_ref[keys, :], query_ref[lanes, :])
    else:
        scores = dot(key_ref[keys, :], query_ref[:, lanes])
    bias = jnp.concatenate([bias_ref[keys, :]] * (BLOCK // LANES), axis=1)
    scores = scores * (LOG2E * width**-0.5) + bias
    if own and keys.start < lanes.stop and lanes.start < keys.stop:
        me = iota(scores.shape, 0) == iota(scores.shape, 1) + (lanes.start - keys.start)
        scores = jnp.where(me, HIDDEN, scores)
    scores_ref[n, keys, :] = scores
    return jnp.max(scores, axis=0, keepdims=True)


def fold(key_ref, query_ref, bias_ref, scores_ref, own, before, finish):
    count = key_ref.shape[0]
    blocks, size = count // BLOCK, PARTS[0 if own else 1]
    parts = [slice(k, k + size) for k in range(0, count, size)]
    peaks, totals = {}, {}
    for n in range(blocks + 1):
        if n < blocks:
            peaks[n], totals[n] = before(n)
            old, new = peaks[n], peaks[n]
        for keys in parts:
            if n < blocks:
                new = jnp.maximum(
                    new, score_part(key_ref, query_ref, bias_ref, scores_ref, n, keys, own)
                )
            if n > 0:
                scores = scores_ref[n - 1, keys, :]
                totals[n - 1] += jnp.sum(jnp.exp2(scores - peaks[n - 1]), axis=0, keepdims=True)
        if n < blocks:
            totals[n] = totals[n] * jnp.exp2(old - new)
            peaks[n] = new
        if n > 0:
            finish(n - 1, peaks[n - 1], totals[n - 1])


def own_kernel(got_ref, turned_ref, peak_ref, total_ref, full_ref, bias_ref, scores_ref):
    full_rows(got_ref, full_ref)
    hide_keys(full_ref, bias_ref)

    def before(n):
        return jnp.full((1, BLOCK), PRIOR, jnp.float32), jnp.ones((1, BLOCK), jnp.float32)

    def finish(n, peak, total):
        peak_ref[:, n * BLOCK : (n + 1) * BLOCK] = peak
        total_ref[:, n * BLOCK : (n + 1) * BLOCK] = total

    fold(full_ref, full_ref, bias_ref, scores_ref, True, before, finish)
    turned_ref[...] = full_ref[...].T


def other_kernel(own_ref, got_ref, peak_ref, total_ref, density_ref, full_ref, bias_ref, scores_ref):
    full_rows(got_ref, full_ref)
    hide_keys(full_ref, bias_ref)

    def before(n):
        lanes = slice(n * BLOCK, (n + 1) * BLOCK)
        return peak_ref[:, lanes], total_ref[:, lanes]

    def finish(n, peak, total):
        density = peak * LN2 + jnp.log(total)
        for v in range(BLOCK // LANES):
            row = density[:, chunk_of(v)].reshape(1, 1, LANES)
            first = (n * BLOCK + v * LANES) // SLOTS
            density_ref[first : first + SHARED] = jnp.broadcast_to(row, (SHARED, 1, LANES))

    fold(full_ref, own_ref, bias_ref, scores_ref, False, before, finish)


def pick_kernel(returned_ref, slot_ref, density_ref):
    owners = returned_ref.shape[0]
    values = returned_ref[...].reshape(owners, LANES)
    slot = slot_ref[...]
    count = slot.shape[1]
    named = (iota((owners, count), 0) == slot // SLOTS).astype(jnp.bfloat16)
    turn = (SHARED - lax.axis_index("gx") % SHARED) % SHARED * SLOTS
    turned = pltpu.roll(values, turn, 1).T[:SLOTS]
    high = turned.astype(jnp.bfloat16)
    left = turned - high.astype(jnp.float32)
    middle = left.astype(jnp.bfloat16)
    low = (left - middle.astype(jnp.float32)).astype(jnp.bfloat16)
    thirds = dot(jnp.concatenate([low, middle, high], axis=0), named)
    picked = (thirds[:SLOTS] + thirds[SLOTS : 2 * SLOTS]) + thirds[2 * SLOTS :]
    mine = iota((SLOTS, count), 0) == slot % SLOTS
    density_ref[...] = jnp.sum(jnp.where(mine, picked, 0.0), axis=0, keepdims=True)


def shards(embeddings, cluster):
    owners = lax.axis_size("gx")
    row_count, width = embeddings.shape
    main = width - LANES
    slot_count = owners * SLOTS
    send, slot = pl.pallas_call(
        pack_kernel,
        in_specs=[ANY_SPEC, ANY_SPEC],
        out_shape=(
            jax.ShapeDtypeStruct((slot_count, main), jnp.bfloat16),
            pltpu.VMEM((1, row_count), jnp.int32),
        ),
        scratch_shapes=[
            pltpu.VMEM((1, row_count), jnp.int32),
            pltpu.VMEM((row_count, width), jnp.bfloat16),
            pltpu.VMEM((slot_count, row_count), jnp.bfloat16),
            pltpu.SemaphoreType.DMA((COPIES + 1,)),
        ],
        compiler_params=PARAMS,
        name="pack",
    )(
        pltpu.with_memory_space_constraint(cluster.reshape(1, row_count), pltpu.HBM),
        pltpu.with_memory_space_constraint(embeddings, pltpu.HBM),
    )
    got = lax.all_to_all(
        send.reshape(owners, SLOTS, main), "gx", split_axis=0, concat_axis=0, tiled=True
    ).reshape(slot_count, main)
    other = lax.ppermute(got, "gy", [(0, 1), (1, 0)])
    own, peak, total = pl.pallas_call(
        own_kernel,
        in_specs=[VMEM_SPEC],
        out_shape=(
            pltpu.VMEM((width, slot_count), jnp.bfloat16),
            pltpu.VMEM((1, slot_count), jnp.float32),
            pltpu.VMEM((1, slot_count), jnp.float32),
        ),
        scratch_shapes=[
            pltpu.VMEM((slot_count, width), jnp.bfloat16),
            pltpu.VMEM((slot_count, LANES), jnp.float32),
            pltpu.VMEM((slot_count // BLOCK, slot_count, BLOCK), jnp.float32),
        ],
        compiler_params=PARAMS,
        name="own",
    )(on_chip(got))
    density = pl.pallas_call(
        other_kernel,
        in_specs=[VMEM_SPEC] * 4,
        out_shape=jax.ShapeDtypeStruct((owners, 1, LANES), jnp.float32),
        scratch_shapes=[
            pltpu.VMEM((slot_count, width), jnp.bfloat16),
            pltpu.VMEM((slot_count, LANES), jnp.float32),
            pltpu.VMEM((slot_count // BLOCK, slot_count, BLOCK), jnp.float32),
        ],
        compiler_params=PARAMS,
        name="other",
    )(on_chip(own), on_chip(other), on_chip(peak), on_chip(total))
    returned = lax.all_to_all(density, "gx", split_axis=0, concat_axis=0, tiled=True)
    picked = pl.pallas_call(
        pick_kernel,
        in_specs=[VMEM_SPEC, VMEM_SPEC],
        out_shape=jax.ShapeDtypeStruct((1, row_count), jnp.float32),
        compiler_params=PARAMS,
        name="pick",
    )(on_chip(returned), on_chip(slot))
    return picked.reshape(row_count)


def solution(mesh):
    return jax.shard_map(
        shards,
        mesh=mesh,
        in_specs=(P(("gx", "gy"), None), P(("gx", "gy"), None)),
        out_specs=P(("gx", "gy")),
        check_vma=False,
    )
```
